32 devices in a mesh: groups: 2 (over x), ctx: 4 (over y, core), head: 4 (over z).
Axes of the slice: x: 2, y: 2, z: 4, core: 2. Of those that a mesh axis runs over, the one named last changes fastest.
Arguments:
- hidden: bfloat16 [2, 2048, 4096], P(None, ('groups', 'ctx'), 'head'), parts along dimension 1, may hold values from -40 to 40
- strand_bases: int32 [2048], P(('groups', 'ctx')), parts along dimension 0, may hold values from 0 to 3
- variant_sites: int32 [256], P('groups'), parts along dimension 0, may hold values from 0 to 1023, as said below
- base_shift: int32 [256], P('groups'), parts along dimension 0, may hold values from 1 to 3
- base_embed: bfloat16 [4, 4096], replicated, may hold values from -6 to 6
- query_weight: bfloat16 [4096, 2048], P(None, 'head')
- key_weight: bfloat16 [4096, 2048], P(None, 'head')
- value_weight: bfloat16 [4096, 2048], P(None, 'head'), may hold values from -0.09375 to 0.09375
- out_weight: bfloat16 [2048, 4096], P('head'), may hold values from -4 to 4
Outputs:
- mixed: bfloat16 [2048, 4096], P(('groups', 'ctx'), 'head'), parts along dimension 0
The draws below stay inside these ranges and needn't reach their ends.
There are 2 independent parts, one for each index of `groups`. The reference program is written for one: setup_inputs(seed, part) draws one part's arguments, and reference() takes and returns one part's arrays. A program takes and returns all parts, laid end to end along the dimension named above; an argument that names none is the same for every part. Nothing has to cross between parts.
Inputs may be any that keep to these rules, and one draw needn't show every extreme that they name: `variant_sites`: distinct positions; each aligned block of 256 positions holds at most 64 of them, and some block holds exactly that many.
All inputs are finite; a program needn't handle non-finite values.
Results may differ from the reference program's by a relative error of at most 0.019.
Values may be sent and summed in bfloat16 or wider, within the bound.
A program may use at most 128 MiB of HBM per device.

```python
import math
import jax
import jax.numpy as jnp
from jax import lax

D = 4096
HEAD_DIM = 128
HEADS = 16
ROWS_DEV = 256
VAR_DEV = 32
SEQ_LEN = 1024
VARS = 128


def draw_hidden(key, part):
    base_draw = jax.random.truncated_normal(jax.random.fold_in(key, 41), -6.0, 6.0, (2, SEQ_LEN, D), jnp.float32)
    base_draw = jnp.clip(base_draw, -40.0, 40.0)
    return base_draw.astype(jnp.bfloat16)


def shared_weights(key):
    head_width = HEADS * HEAD_DIM
    shared = jax.random.truncated_normal(jax.random.fold_in(key, 31), -4.0, 4.0, (D, head_width), jnp.float32) / math.sqrt(D)
    private = jax.random.truncated_normal(jax.random.fold_in(key, 32), -4.0, 4.0, (D, head_width), jnp.float32) / math.sqrt(D)
    return (shared, private)


def draw_query_weight(key, part):
    shared, private = shared_weights(key)
    return shared.astype(jnp.bfloat16)


def draw_key_weight(key, part):
    shared, private = shared_weights(key)
    result = private
    return result.astype(jnp.bfloat16)


def draw_variant_sites(key, part):
    block_total = SEQ_LEN // ROWS_DEV
    slot_cap = 2 * VAR_DEV
    key_order = jax.random.fold_in(key, 51)
    key_shift = jax.random.fold_in(key, 52)
    key_rows = jax.random.fold_in(key, 53)
    key_mix = jax.random.fold_in(key, 54)
    block_order = jax.random.permutation(key_order, block_total)
    shifts = jax.random.randint(key_shift, (block_total // 2,), 0, VAR_DEV + 1)
    shifts = shifts.at[0].set(VAR_DEV)
    signed = jnp.concatenate([shifts, -shifts])
    counts = jnp.zeros((block_total,), jnp.int32).at[block_order].set(VAR_DEV + signed)
    row_keys = jax.random.split(key_rows, block_total)
    row_perm = jax.vmap(lambda sub_key: jax.random.permutation(sub_key, ROWS_DEV))(row_keys)[:, :slot_cap]
    positions = (jnp.arange(block_total, dtype=jnp.int32)[:, None] * ROWS_DEV + row_perm).reshape(-1)
    is_valid = (jnp.arange(slot_cap, dtype=jnp.int32)[None, :] < counts[:, None]).reshape(-1)
    ranked = jnp.argsort(jnp.where(is_valid, 0, 1), stable=True)[:VARS]
    chosen = positions[ranked]
    shuffle = jax.random.permutation(key_mix, VARS)
    return chosen[shuffle].astype(jnp.int32)


def touch_ends(values, own_key, low, high):
    index_at = [jax.random.randint(jax.random.fold_in(own_key, axis), (), 0, length) for axis, length in enumerate(values.shape)]
    main_axis = values.shape.index(max(values.shape))
    beside = index_at[:main_axis] + [(index_at[main_axis] + 1) % values.shape[main_axis]] + index_at[main_axis + 1:]
    return values.at[tuple(index_at)].set(low).at[tuple(beside)].set(high)


def shard_levels(own_key, shape, shards, least, top_value):
    def one(axis_at, shards_of):
        draws = jax.random.uniform(jax.random.fold_in(jax.random.fold_in(own_key, 6), axis_at), (shards_of,), jnp.float32, least / len(shards), top_value / len(shards))
        return jnp.repeat(jnp.exp(draws), shape[axis_at] // shards_of).reshape((-1,) + (1,) * (len(shape) - axis_at - 1))

    factor_of = one(*shards[0])
    for cut in shards[1:]:
        factor_of = factor_of * one(*cut)
    return factor_of


def bell_draw(stream_key, shape, deviation, limit, cuts=(), kind=jnp.bfloat16):
    array = deviation * jax.random.normal(stream_key, shape, jnp.float32)
    if cuts:
        array = array * shard_levels(stream_key, shape, cuts, -0.22, 0.18)
    return jnp.clip(array, -limit, limit).astype(kind)


def setup_inputs(seed: int = 0, part: int = 0) -> dict:
    arg_keys = jax.random.split(jax.random.key(seed), 10)
    own_keys = jax.random.split(jax.random.fold_in(arg_keys[9], part), 10)
    hidden = draw_hidden(jax.random.fold_in(jax.random.fold_in(arg_keys[9], part), 71), part)
    strand_bases = touch_ends(jax.random.randint(own_keys[1], (SEQ_LEN,), 0, 4), jax.random.fold_in(own_keys[1], 1), 0, 3).astype(jnp.int32)
    variant_sites = draw_variant_sites(jax.random.fold_in(jax.random.fold_in(arg_keys[9], part), 71), part)
    base_shift = touch_ends(jax.random.randint(own_keys[3], (VARS,), 1, 4), jax.random.fold_in(own_keys[3], 1), 1, 3).astype(jnp.int32)
    base_embed = bell_draw(arg_keys[4], (4, D), 1.0, 6.0)
    query_weight = draw_query_weight(jax.random.fold_in(arg_keys[9], 71), part)
    key_weight = draw_key_weight(jax.random.fold_in(arg_keys[9], 71), part)
    value_weight = bell_draw(arg_keys[7], (D, HEADS * HEAD_DIM), D ** -0.5, 0.09375, ((1, 4),))
    out_weight = bell_draw(arg_keys[8], (HEADS * HEAD_DIM, D), 2 ** -0.5, 4.0, ((0, 4),))
    return dict(hidden=hidden, strand_bases=strand_bases, variant_sites=variant_sites, base_shift=base_shift, base_embed=base_embed, query_weight=query_weight, key_weight=key_weight, value_weight=value_weight, out_weight=out_weight)


ROPE_BASE = 10000.0

def rotate(values, positions):
    half_dim = values.shape[-1] // 2
    freq_table = jnp.power(ROPE_BASE, -jnp.arange(half_dim, dtype=jnp.float32) * 2.0 / values.shape[-1])
    angle_grid = positions[:, None] * freq_table[None, :]
    cos_part = jnp.cos(angle_grid)[:, None, :]
    sin_part = jnp.sin(angle_grid)[:, None, :]
    lower_half = values[..., :half_dim]
    upper_half = values[..., half_dim:]
    return jnp.concatenate([lower_half * cos_part - upper_half * sin_part, upper_half * cos_part + lower_half * sin_part], axis=-1)

def project_rows(inputs, weight, positions, rotated):
    n_rows = inputs.shape[0]
    product = jnp.dot(inputs, weight, preferred_element_type=jnp.float32)
    product = product.reshape(n_rows, -1, HEAD_DIM)
    if rotated:
        product = rotate(product, positions)
    return product.astype(jnp.bfloat16)

def attend(queries, keys_in, values_in, forward):
    window_iota = jnp.arange(SEQ_LEN, dtype=jnp.int32)
    if forward:
        allowed = window_iota[None, :] <= window_iota[:, None]
    else:
        allowed = window_iota[None, :] >= window_iota[:, None]

    def one_head(operands):
        head_query, head_key, head_value = operands
        scores = jnp.dot(head_query, head_key.T, preferred_element_type=jnp.float32) / math.sqrt(HEAD_DIM)
        masked = jnp.where(allowed, scores, -jnp.inf)
        row_max = lax.optimization_barrier(jnp.max(masked, axis=1, keepdims=True))
        weights = jnp.where(allowed, jnp.exp(scores - row_max), 0.0)
        weights = weights / lax.optimization_barrier(jnp.sum(weights, axis=1, keepdims=True))
        return jnp.dot(weights.astype(jnp.bfloat16), head_value, preferred_element_type=jnp.float32)
    return lax.map(one_head, (queries.transpose(1, 0, 2), keys_in.transpose(1, 0, 2), values_in.transpose(1, 0, 2)))

def reference(hidden, strand_bases, variant_sites, base_shift, base_embed, query_weight, key_weight, value_weight, out_weight):
    embed_table = base_embed.astype(jnp.float32)
    old_base = strand_bases[variant_sites]
    new_base = (old_base + base_shift) % 4
    plus_diff = embed_table[new_base] - embed_table[old_base]
    minus_diff = embed_table[3 - new_base] - embed_table[3 - old_base]
    window_pos = jnp.arange(SEQ_LEN, dtype=jnp.float32)
    plus_pos = window_pos
    minus_pos = SEQ_LEN - 1 - window_pos
    plus_rows = (hidden[0][variant_sites].astype(jnp.float32) + plus_diff).astype(jnp.bfloat16)
    minus_rows = (hidden[1][variant_sites].astype(jnp.float32) + minus_diff).astype(jnp.bfloat16)
    mutant_plus = hidden[0].at[variant_sites].set(plus_rows)
    mutant_minus = hidden[1].at[variant_sites].set(minus_rows)
    outcomes = []
    for inputs, positions, forward in ((hidden[0], plus_pos, True), (mutant_plus, plus_pos, True), (hidden[1], minus_pos, False), (mutant_minus, minus_pos, False)):
        queries = project_rows(inputs, query_weight, positions, True)
        keys_out = project_rows(inputs, key_weight, positions, True)
        values_out = project_rows(inputs, value_weight, positions, False)
        outcomes.append(attend(queries, keys_out, values_out, forward))
    combined = 0.5 * (outcomes[0] - outcomes[1] + (outcomes[2] - outcomes[3]))
    combined = combined.transpose(1, 0, 2).reshape(SEQ_LEN, -1).astype(jnp.bfloat16)
    return jnp.dot(combined, out_weight, preferred_element_type=jnp.float32).astype(jnp.bfloat16)
```

```python
import functools
import math

import jax
import jax.numpy as jnp
from jax import lax
from jax.experimental import pallas as pl
from jax.experimental.pallas import tpu as pltpu
from jax.sharding import PartitionSpec as P

HEAD_DIM = 128
VAR_DEV = 32
ROPE_BASE = 10000.0
NEG_FILL = -1e30
FAR = 1 << 29
PIECES = 2
MESH = pl.DeviceIdType.MESH
VMEM_LIMIT = 60 * 1024 * 1024


def greet(axis, size):
    me = lax.axis_index(axis)
    barrier = pltpu.get_barrier_semaphore()

    @pl.when(me > 0)
    def _():
        pl.semaphore_signal(barrier, inc=1, device_id={axis: me - 1}, device_id_type=MESH)

    @pl.when(me < size - 1)
    def _():
        pl.semaphore_signal(barrier, inc=1, device_id={axis: me + 1}, device_id_type=MESH)

    pl.semaphore_wait(barrier, jnp.minimum(me, 1) + jnp.minimum(size - 1 - me, 1))


def project_kernel(
    size,
    hidden,
    wq,
    wk,
    wv,
    sel,
    sel_t,
    has_row,
    codes,
    table,
    cos,
    sin,
    q_out,
    kv_out,
    xbuf,
    wbuf,
    stk,
    acc,
    own_sem,
    w_sem,
    s_sem,
    r_sem,
):
    z = lax.axis_index("head")
    rows, feats = hidden.shape[1], hidden.shape[2]
    slots = sel.shape[0]
    hw = wq.shape[1]
    heads = hw // HEAD_DIM
    piece = rows // PIECES

    greet("head", size)

    def hop(side, strand, shard, part, source):
        span = pl.ds(part * piece, piece)
        return pltpu.make_async_remote_copy(
            src_ref=source.at[strand, span] if source is hidden else xbuf.at[strand, shard, span],
            dst_ref=xbuf.at[strand, shard, span],
            send_sem=s_sem.at[side, strand, shard, part],
            recv_sem=r_sem.at[strand, shard, part],
            device_id={"head": z - 1 if side == 0 else z + 1},
            device_id_type=MESH,
        )

    def send_own(side, strand):
        for part in range(PIECES):
            hop(side, strand, z, part, hidden).start()

    for strand in range(1):

        @pl.when(z > 0)
        def _():
            send_own(0, strand)

        @pl.when(z < size - 1)
        def _():
            send_own(1, strand)

    @pl.when((z > 0) & (z == size - 1))
    def _():
        send_own(0, 1)

    @pl.when((z < size - 1) & (z == 0))
    def _():
        send_own(1, 1)

    own = [
        pltpu.make_async_copy(hidden.at[strand], xbuf.at[strand, z], own_sem.at[strand])
        for strand in range(2)
    ]
    loads = [
        pltpu.make_async_copy(weight, wbuf.at[index], w_sem.at[index])
        for index, weight in enumerate((wq, wk, wv))
    ]
    for copy in own + loads:
        copy.start()
    for copy in own + loads:
        copy.wait()

    shorter = jnp.minimum(z, size - 1 - z)
    long_side = jnp.where(z < size - 1 - z, 1, -1)

    def shard_of(step):
        paired = jnp.where(step % 2 == 1, (step + 1) // 2, -((step + 1) // 2))
        return z + jnp.where(step <= 2 * shorter, paired, long_side * (step - shorter))

    for strand in range(2):
        acc[...] = jnp.zeros_like(acc)

        def step_body(step, carry):
            shard = shard_of(step)
            for part in range(PIECES):

                @pl.when(shard > z)
                def _():
                    hop(0, strand, shard, part, xbuf).wait_recv()

                    @pl.when(z > 0)
                    def _():
                        hop(0, strand, shard, part, xbuf).start()

                @pl.when(shard < z)
                def _():
                    hop(1, strand, shard, part, xbuf).wait_recv()

                    @pl.when(z < size - 1)
                    def _():
                        hop(1, strand, shard, part, xbuf).start()

            if strand == 0:

                @pl.when((shard == size - 1) & (z < size - 1) & (z > 0))
                def _():
                    send_own(0, 1)

                @pl.when((shard == 0) & (z > 0) & (z < size - 1))
                def _():
                    send_own(1, 1)

            block = xbuf[strand, shard]
            stk[pl.ds(0, rows), :] = block
            first = pl.multiple_of(shard * feats, feats)
            diff = jnp.zeros((slots, feats), jnp.float32)
            for code in range(4):
                diff = diff + codes[strand][:, code : code + 1] * table[
                    pl.ds(code, 1), pl.ds(first, feats)
                ]
            picked = jnp.dot(sel[...], block, preferred_element_type=jnp.float32)
            stk[pl.ds(rows, slots), :] = (picked + diff).astype(jnp.bfloat16)
            for index in range(3):
                acc[:, pl.ds(index * hw, hw)] += jnp.dot(
                    stk[...],
                    wbuf[index, pl.ds(first, feats), :],
                    preferred_element_type=jnp.float32,
                )
            return carry

        lax.fori_loop(0, size, step_body, 0)

        cos_part = cos[strand]
        sin_part = sin[strand]
        for head in range(heads):
            cols = pl.ds(head * HEAD_DIM, HEAD_DIM)
            for index in range(2):
                raw = acc[:, pl.ds(index * hw + head * HEAD_DIM, HEAD_DIM)]
                turned = raw * cos_part + pltpu.roll(raw, HEAD_DIM // 2, 1) * sin_part
                turned = turned.astype(jnp.bfloat16)
                if index == 0:
                    base = turned[:rows]
                    placed = jnp.dot(
                        sel_t[...], turned[rows:], preferred_element_type=jnp.float32
                    )
                    q_out[strand, 0, :, cols] = base
                    q_out[strand, 1, :, cols] = jnp.where(
                        has_row[...] > 0.5, placed, base.astype(jnp.float32)
                    ).astype(jnp.bfloat16)
                else:
                    kv_out[strand, :, cols] = turned
        kv_out[strand, :, pl.ds(hw, hw)] = acc[:, pl.ds(2 * hw, hw)].astype(jnp.bfloat16)

    def drain(step, carry):
        shard = shard_of(step)
        for strand in range(2):
            for part in range(PIECES):

                @pl.when((shard >= z) & (z > 0))
                def _():
                    hop(0, strand, shard, part, xbuf).wait_send()

                @pl.when((shard <= z) & (z < size - 1))
                def _():
                    hop(1, strand, shard, part, xbuf).wait_send()

        return carry

    lax.fori_loop(0, size, drain, 0)


def attend_kernel(size, q_in, kv_in, kt_mut, out, kvbuf, m_buf, l_buf, a_buf, s_sem, r_sem):
    me = lax.axis_index("ctx")
    rows, hw = q_in.shape[2], q_in.shape[3]
    heads = hw // HEAD_DIM
    wide = kv_in.shape[1]
    window = rows * size
    log_scale = math.log2(math.e) / math.sqrt(HEAD_DIM)

    greet("ctx", size)

    def hop(strand, shard, own):
        return pltpu.make_async_remote_copy(
            src_ref=kv_in.at[strand] if own else kvbuf.at[strand, shard],
            dst_ref=kvbuf.at[strand, shard],
            send_sem=s_sem.at[strand, shard],
            recv_sem=r_sem.at[strand, shard],
            device_id={"ctx": me + 1 if strand == 0 else me - 1},
            device_id_type=MESH,
        )

    passes_on = (me < size - 1, me > 0)
    for strand in range(2):

        @pl.when(passes_on[strand])
        def _():
            hop(strand, me, True).start()

    row_iota = lax.broadcasted_iota(jnp.int32, (rows, 1), 0)
    col_iota = lax.broadcasted_iota(jnp.int32, (1, rows), 1)

    def clock(strand, block, iota):
        place = block * rows + iota
        return place if strand == 0 else window - 1 - place

    def update(strand, shard, block, first):
        q_time = clock(strand, me, row_iota)
        k_times = (clock(strand, shard, col_iota), kt_mut[strand, shard])
        spans = (rows, wide)

        def one_head(head, carry):
            k_cols = pl.ds(pl.multiple_of(head * HEAD_DIM, HEAD_DIM), HEAD_DIM)
            v_cols = pl.ds(pl.multiple_of(hw + head * HEAD_DIM, HEAD_DIM), HEAD_DIM)
            for kind in range(2):
                span = pl.ds(0, spans[kind])
                raw = lax.dot_general(
                    q_in[strand, kind, :, k_cols],
                    block[span, k_cols],
                    (((1,), (1,)), ((), ())),
                    preferred_element_type=jnp.float32,
                )
                raw = jnp.where(k_times[kind] <= q_time, raw, NEG_FILL)
                top = jnp.max(raw, axis=1, keepdims=True)
                if not first:
                    old = m_buf[strand, head, kind]
                    top = jnp.maximum(old, top)
                    fade = jnp.exp2((old - top) * log_scale)
                weights = jnp.exp2((raw - top) * log_scale)
                total = jnp.sum(weights, axis=1, keepdims=True)
                vec = jnp.dot(
                    weights.astype(jnp.bfloat16),
                    block[span, v_cols],
                    preferred_element_type=jnp.float32,
                )
                if not first:
                    total = total + fade * l_buf[strand, head, kind]
                    vec = vec + fade * a_buf[strand, head, kind]
                m_buf[strand, head, kind] = top
                l_buf[strand, head, kind] = total
                a_buf[strand, head, kind] = vec
            return carry

        lax.fori_loop(0, heads, one_head, 0)

    for strand in range(2):
        update(strand, me, kv_in.at[strand], True)

    def arrive(step, carry):
        shards = (me - step, me + step)
        live = (me - step >= 0, me + step < size)
        for strand in range(2):

            @pl.when(live[strand])
            def _():
                hop(strand, shards[strand], False).wait_recv()

                @pl.when(passes_on[strand])
                def _():
                    hop(strand, shards[strand], False).start()

                update(strand, shards[strand], kvbuf.at[strand, shards[strand]], False)

        return carry

    lax.fori_loop(1, size, arrive, 0)

    for head in range(heads):
        part = [
            a_buf[strand, head, kind] / l_buf[strand, head, kind]
            for strand in range(2)
            for kind in range(2)
        ]
        out[:, pl.ds(head * HEAD_DIM, HEAD_DIM)] = (
            0.5 * ((part[0] - part[1]) + (part[2] - part[3]))
        ).astype(jnp.bfloat16)

    def drain(step, carry):
        shards = (me - step, me + step)
        live = (me - step >= 0, me + step < size)
        for strand in range(2):

            @pl.when(live[strand] & passes_on[strand])
            def _():
                hop(strand, shards[strand], False).wait_send()

        return carry

    lax.fori_loop(0, size, drain, 0)


def vmem():
    return pl.BlockSpec(memory_space=pltpu.VMEM)


def anywhere():
    return pl.BlockSpec(memory_space=pl.ANY)


def shards(
    hidden,
    strand_bases,
    variant_sites,
    base_shift,
    base_embed,
    query_weight,
    key_weight,
    value_weight,
    out_weight,
):
    rows, feats = hidden.shape[1], hidden.shape[2]
    n_head = lax.axis_size("head")
    n_ctx = lax.axis_size("ctx")
    window = rows * n_ctx
    me = lax.axis_index("ctx")
    start = me * rows
    slots = 2 * VAR_DEV
    wide = rows + slots
    hw = query_weight.shape[1]
    heads = hw // HEAD_DIM
    width = query_weight.shape[0]

    count = variant_sites.shape[0]
    order = jnp.arange(count, dtype=jnp.int32)
    row_iota = jnp.arange(rows, dtype=jnp.int32)
    v_block = variant_sites // rows
    before = (v_block[:, None] == v_block[None, :]) & (order[None, :] < order[:, None])
    rank = jnp.sum(before.astype(jnp.int32), axis=1)
    mine = v_block == me
    slot_iota = jnp.arange(slots, dtype=jnp.int32)
    slot_match = (rank[:, None] == slot_iota[None, :]) & mine[:, None]
    row_match = ((variant_sites - start)[:, None] == row_iota[None, :]) & mine[:, None]
    old_base = jnp.sum(jnp.where(row_match, strand_bases[None, :], 0), axis=1)
    new_base = jnp.mod(old_base + base_shift, 4)
    slot_old = jnp.sum(jnp.where(slot_match, old_base[:, None], 0), axis=0)
    slot_new = jnp.sum(jnp.where(slot_match, new_base[:, None], 0), axis=0)
    slot_live = jnp.any(slot_match, axis=0)
    has_row = jnp.any(row_match, axis=0).astype(jnp.float32)[:, None]

    all_slot = v_block * slots + rank
    all_match = all_slot[:, None] == jnp.arange(n_ctx * slots, dtype=jnp.int32)[None, :]
    all_pos = jnp.sum(jnp.where(all_match, variant_sites[:, None], 0), axis=0)
    all_live = jnp.any(all_match, axis=0)
    slot_pos = jnp.sum(jnp.where(slot_match, variant_sites[:, None], 0), axis=0)
    place = jnp.arange(window, dtype=jnp.int32)
    has_key = jnp.any(variant_sites[:, None] == place[None, :], axis=0)
    kt_mut = jnp.stack(
        [
            jnp.concatenate(
                [
                    jnp.where(has_key, FAR, flip(place)).reshape(n_ctx, rows),
                    jnp.where(all_live, flip(all_pos), FAR).reshape(n_ctx, slots),
                ],
                axis=1,
            )
            for flip in (lambda p: p, lambda p: window - 1 - p)
        ]
    )[:, :, None, :]

    sel = (
        (jnp.where(slot_live, slot_pos - start, -1)[:, None] == row_iota[None, :])
    ).astype(jnp.bfloat16)
    sel_t = (
        (row_iota[:, None] == jnp.where(slot_live, slot_pos - start, -1)[None, :])
    ).astype(jnp.bfloat16)
    code_iota = jnp.arange(4, dtype=jnp.int32)

    def signed(new, old):
        hot = (new[:, None] == code_iota[None, :]).astype(jnp.float32) - (
            old[:, None] == code_iota[None, :]
        ).astype(jnp.float32)
        return jnp.where(slot_live[:, None], hot, 0.0)

    codes = jnp.stack([signed(slot_new, slot_old), signed(3 - slot_new, 3 - slot_old)])
    table = base_embed.astype(jnp.float32)

    plus_pos = jnp.concatenate([start + row_iota, slot_pos])
    pos = jnp.stack([plus_pos, window - 1 - plus_pos]).astype(jnp.float32)
    half = HEAD_DIM // 2
    freq = jnp.power(ROPE_BASE, -jnp.arange(half, dtype=jnp.float32) * 2.0 / HEAD_DIM)
    angle = pos[:, :, None] * freq[None, None, :]
    cos_half, sin_half = jnp.cos(angle), jnp.sin(angle)
    cos = jnp.concatenate([cos_half, cos_half], axis=-1)
    sin = jnp.concatenate([-sin_half, sin_half], axis=-1)

    queries, cache = pl.pallas_call(
        functools.partial(project_kernel, n_head),
        out_shape=(
            jax.ShapeDtypeStruct((2, 2, rows, hw), jnp.bfloat16),
            jax.ShapeDtypeStruct((2, wide, 2 * hw), jnp.bfloat16),
        ),
        in_specs=[anywhere()] * 4 + [vmem()] * 7,
        out_specs=(vmem(), vmem()),
        scratch_shapes=[
            pltpu.VMEM((2, n_head, rows, feats), jnp.bfloat16),
            pltpu.VMEM((3, width, hw), jnp.bfloat16),
            pltpu.VMEM((wide, feats), jnp.bfloat16),
            pltpu.VMEM((wide, 3 * hw), jnp.float32),
            pltpu.SemaphoreType.DMA((2,)),
            pltpu.SemaphoreType.DMA((3,)),
            pltpu.SemaphoreType.DMA((2, 2, n_head, PIECES)),
            pltpu.SemaphoreType.DMA((2, n_head, PIECES)),
        ],
        compiler_params=pltpu.CompilerParams(
            collective_id=0, has_side_effects=True, vmem_limit_bytes=VMEM_LIMIT
        ),
        name="project",
    )(
        hidden,
        query_weight,
        key_weight,
        value_weight,
        sel,
        sel_t,
        has_row,
        codes,
        table,
        cos,
        sin,
    )

    combined = pl.pallas_call(
        functools.partial(attend_kernel, n_ctx),
        out_shape=jax.ShapeDtypeStruct((rows, hw), jnp.bfloat16),
        in_specs=[vmem()] * 3,
        out_specs=vmem(),
        scratch_shapes=[
            pltpu.VMEM((2, n_ctx, wide, 2 * hw), jnp.bfloat16),
            pltpu.VMEM((2, heads, 2, rows, 1), jnp.float32),
            pltpu.VMEM((2, heads, 2, rows, 1), jnp.float32),
            pltpu.VMEM((2, heads, 2, rows, HEAD_DIM), jnp.float32),
            pltpu.SemaphoreType.DMA((2, n_ctx)),
            pltpu.SemaphoreType.DMA((2, n_ctx)),
        ],
        compiler_params=pltpu.CompilerParams(
            collective_id=1, has_side_effects=True, vmem_limit_bytes=VMEM_LIMIT
        ),
        name="attend",
    )(queries, cache, kt_mut)

    summed = lax.psum_scatter(
        lax.dot_general(
            out_weight, combined, (((0,), (1,)), ((), ())), preferred_element_type=jnp.float32
        ).astype(jnp.bfloat16),
        "head",
        scatter_dimension=0,
        tiled=True,
    ).astype(jnp.float32)
    return summed.T.astype(jnp.bfloat16)


def solution(mesh):
    return jax.shard_map(
        shards,
        mesh=mesh,
        in_specs=(
            P(None, ("groups", "ctx"), "head"),
            P(("groups", "ctx")),
            P("groups"),
            P("groups"),
            P(),
            P(None, "head"),
            P(None, "head"),
            P(None, "head"),
            P("head", None),
        ),
        out_specs=P(("groups", "ctx"), "head"),
        check_vma=False,
    )
```

```python
import functools
import math

import jax
import jax.numpy as jnp
from jax import lax
from jax.experimental import pallas as pl
from jax.experimental.pallas import tpu as pltpu
from jax.sharding import PartitionSpec as P

HEAD_DIM = 128
VAR_DEV = 32
ROPE_BASE = 10000.0
NEG_FILL = -1e30
FAR = 1 << 29
PIECES = 2
MESH = pl.DeviceIdType.MESH
VMEM_LIMIT = 60 * 1024 * 1024


def greet(*axes):
    barrier = pltpu.get_barrier_semaphore()
    peers = 0
    for axis, size in axes:
        me = lax.axis_index(axis)

        @pl.when(me > 0)
        def _():
            pl.semaphore_signal(barrier, inc=1, device_id={axis: me - 1}, device_id_type=MESH)

        @pl.when(me < size - 1)
        def _():
            pl.semaphore_signal(barrier, inc=1, device_id={axis: me + 1}, device_id_type=MESH)

        peers = peers + jnp.minimum(me, 1) + jnp.minimum(size - 1 - me, 1)
    pl.semaphore_wait(barrier, peers)


def near_first(z, size):
    shorter = jnp.minimum(z, size - 1 - z)
    long_side = jnp.where(z < size - 1 - z, 1, -1)

    def shard_of(step):
        paired = jnp.where(step % 2 == 1, (step + 1) // 2, -((step + 1) // 2))
        return z + jnp.where(step <= 2 * shorter, paired, long_side * (step - shorter))

    return shard_of


def project_kernel(
    size,
    hidden,
    wq,
    wk,
    wv,
    sel,
    sel_t,
    has_row,
    codes,
    table,
    cos,
    sin,
    q_out,
    kv_out,
    xbuf,
    wbuf,
    stk,
    acc,
    own_sem,
    w_sem,
    s_sem,
    r_sem,
):
    z = lax.axis_index("head")
    rows, feats = hidden.shape[1], hidden.shape[2]
    slots = sel.shape[0]
    hw = wq.shape[1]
    heads = hw // HEAD_DIM
    piece = rows // PIECES

    greet(("head", size))

    def hop(side, strand, shard, part, source):
        span = pl.ds(part * piece, piece)
        return pltpu.make_async_remote_copy(
            src_ref=source.at[strand, span] if source is hidden else xbuf.at[strand, shard, span],
            dst_ref=xbuf.at[strand, shard, span],
            send_sem=s_sem.at[side, strand, shard, part],
            recv_sem=r_sem.at[strand, shard, part],
            device_id={"head": z - 1 if side == 0 else z + 1},
            device_id_type=MESH,
        )

    def send_own(side, strand):
        for part in range(PIECES):
            hop(side, strand, z, part, hidden).start()

    for strand in range(1):

        @pl.when(z > 0)
        def _():
            send_own(0, strand)

        @pl.when(z < size - 1)
        def _():
            send_own(1, strand)

    @pl.when((z > 0) & (z == size - 1))
    def _():
        send_own(0, 1)

    @pl.when((z < size - 1) & (z == 0))
    def _():
        send_own(1, 1)

    own = [
        pltpu.make_async_copy(hidden.at[strand], xbuf.at[strand, z], own_sem.at[strand])
        for strand in range(2)
    ]
    loads = [
        pltpu.make_async_copy(weight, wbuf.at[index], w_sem.at[index])
        for index, weight in enumerate((wq, wk, wv))
    ]
    for copy in own + loads:
        copy.start()
    for copy in own + loads:
        copy.wait()

    shard_of = near_first(z, size)

    for strand in range(2):
        acc[...] = jnp.zeros_like(acc)

        def step_body(step, carry):
            shard = shard_of(step)
            for part in range(PIECES):

                @pl.when(shard > z)
                def _():
                    hop(0, strand, shard, part, xbuf).wait_recv()

                    @pl.when(z > 0)
                    def _():
                        hop(0, strand, shard, part, xbuf).start()

                @pl.when(shard < z)
                def _():
                    hop(1, strand, shard, part, xbuf).wait_recv()

                    @pl.when(z < size - 1)
                    def _():
                        hop(1, strand, shard, part, xbuf).start()

            if strand == 0:

                @pl.when((shard == size - 1) & (z < size - 1) & (z > 0))
                def _():
                    send_own(0, 1)

                @pl.when((shard == 0) & (z > 0) & (z < size - 1))
                def _():
                    send_own(1, 1)

            block = xbuf[strand, shard]
            stk[pl.ds(0, rows), :] = block
            first = pl.multiple_of(shard * feats, feats)
            diff = jnp.zeros((slots, feats), jnp.float32)
            for code in range(4):
                diff = diff + codes[strand][:, code : code + 1] * table[
                    pl.ds(code, 1), pl.ds(first, feats)
                ]
            picked = jnp.dot(sel[...], block, preferred_element_type=jnp.float32)
            stk[pl.ds(rows, slots), :] = (picked + diff).astype(jnp.bfloat16)
            for index in range(3):
                acc[:, pl.ds(index * hw, hw)] += jnp.dot(
                    stk[...],
                    wbuf[index, pl.ds(first, feats), :],
                    preferred_element_type=jnp.float32,
                )
            return carry

        lax.fori_loop(0, size, step_body, 0)

        cos_part = cos[strand]
        sin_part = sin[strand]
        for head in range(heads):
            cols = pl.ds(head * HEAD_DIM, HEAD_DIM)
            for index in range(2):
                raw = acc[:, pl.ds(index * hw + head * HEAD_DIM, HEAD_DIM)]
                turned = raw * cos_part + pltpu.roll(raw, HEAD_DIM // 2, 1) * sin_part
                turned = turned.astype(jnp.bfloat16)
                if index == 0:
                    base = turned[:rows]
                    placed = jnp.dot(
                        sel_t[...], turned[rows:], preferred_element_type=jnp.float32
                    )
                    q_out[strand, 0, :, cols] = base
                    q_out[strand, 1, :, cols] = jnp.where(
                        has_row[...] > 0.5, placed, base.astype(jnp.float32)
                    ).astype(jnp.bfloat16)
                else:
                    kv_out[strand, :, cols] = turned
        kv_out[strand, :, pl.ds(hw, hw)] = acc[:, pl.ds(2 * hw, hw)].astype(jnp.bfloat16)

    def drain(step, carry):
        shard = shard_of(step)
        for strand in range(2):
            for part in range(PIECES):

                @pl.when((shard >= z) & (z > 0))
                def _():
                    hop(0, strand, shard, part, xbuf).wait_send()

                @pl.when((shard <= z) & (z < size - 1))
                def _():
                    hop(1, strand, shard, part, xbuf).wait_send()

        return carry

    lax.fori_loop(0, size, drain, 0)


def attend_kernel(
    size,
    n_head,
    q_in,
    kv_in,
    kt_mut,
    w_in,
    out,
    kvbuf,
    m_buf,
    l_buf,
    a_buf,
    w_buf,
    gbuf,
    mine,
    total_out,
    s_sem,
    r_sem,
    w_sem,
    gs_sem,
    gr_sem,
):
    me = lax.axis_index("ctx")
    z = lax.axis_index("head")
    rows, hw = q_in.shape[2], q_in.shape[3]
    heads = hw // HEAD_DIM
    wide = kv_in.shape[1]
    window = rows * size
    log_scale = math.log2(math.e) / math.sqrt(HEAD_DIM)

    greet(("ctx", size), ("head", n_head))
    w_load = pltpu.make_async_copy(w_in, w_buf, w_sem)
    w_load.start()

    def hop(strand, shard, own):
        return pltpu.make_async_remote_copy(
            src_ref=kv_in.at[strand] if own else kvbuf.at[strand, shard],
            dst_ref=kvbuf.at[strand, shard],
            send_sem=s_sem.at[strand, shard],
            recv_sem=r_sem.at[strand, shard],
            device_id={"ctx": me + 1 if strand == 0 else me - 1},
            device_id_type=MESH,
        )

    passes_on = (me < size - 1, me > 0)
    for strand in range(2):

        @pl.when(passes_on[strand])
        def _():
            hop(strand, me, True).start()

    row_iota = lax.broadcasted_iota(jnp.int32, (rows, 1), 0)
    col_iota = lax.broadcasted_iota(jnp.int32, (1, rows), 1)

    def clock(strand, block, iota):
        place = block * rows + iota
        return place if strand == 0 else window - 1 - place

    def update(strand, shard, block, first):
        q_time = clock(strand, me, row_iota)
        k_times = (clock(strand, shard, col_iota), kt_mut[strand, shard])
        spans = (rows, wide)

        def one_head(head, carry):
            k_cols = pl.ds(pl.multiple_of(head * HEAD_DIM, HEAD_DIM), HEAD_DIM)
            v_cols = pl.ds(pl.multiple_of(hw + head * HEAD_DIM, HEAD_DIM), HEAD_DIM)
            for kind in range(2):
                span = pl.ds(0, spans[kind])
                raw = lax.dot_general(
                    q_in[strand, kind, :, k_cols],
                    block[span, k_cols],
                    (((1,), (1,)), ((), ())),
                    preferred_element_type=jnp.float32,
                )
                raw = jnp.where(k_times[kind] <= q_time, raw, NEG_FILL)
                top = jnp.max(raw, axis=1, keepdims=True)
                if not first:
                    old = m_buf[strand, head, kind]
                    top = jnp.maximum(old, top)
                    fade = jnp.exp2((old - top) * log_scale)
                weights = jnp.exp2((raw - top) * log_scale)
                total = jnp.sum(weights, axis=1, keepdims=True)
                vec = jnp.dot(
                    weights.astype(jnp.bfloat16),
                    block[span, v_cols],
                    preferred_element_type=jnp.float32,
                )
                if not first:
                    total = total + fade * l_buf[strand, head, kind]
                    vec = vec + fade * a_buf[strand, head, kind]
                m_buf[strand, head, kind] = top
                l_buf[strand, head, kind] = total
                a_buf[strand, head, kind] = vec
            return carry

        lax.fori_loop(0, heads, one_head, 0)

    for strand in range(2):
        update(strand, me, kv_in.at[strand], True)

    def arrive(step, carry):
        shards = (me - step, me + step)
        live = (me - step >= 0, me + step < size)
        for strand in range(2):

            @pl.when(live[strand])
            def _():
                hop(strand, shards[strand], False).wait_recv()

                @pl.when(passes_on[strand])
                def _():
                    hop(strand, shards[strand], False).start()

                update(strand, shards[strand], kvbuf.at[strand, shards[strand]], False)

        return carry

    lax.fori_loop(1, size, arrive, 0)

    def pass_on(side, shard, head, own):
        return pltpu.make_async_remote_copy(
            src_ref=mine.at[head] if own else gbuf.at[shard, head],
            dst_ref=gbuf.at[shard, head],
            send_sem=gs_sem.at[side, shard, head],
            recv_sem=gr_sem.at[shard, head],
            device_id={"head": z - 1 if side == 0 else z + 1},
            device_id_type=MESH,
        )

    for head in range(heads):
        part = [
            a_buf[strand, head, kind] / l_buf[strand, head, kind]
            for strand in range(2)
            for kind in range(2)
        ]
        mine[head] = (0.5 * ((part[0] - part[1]) + (part[2] - part[3]))).astype(jnp.bfloat16)

        @pl.when(z > 0)
        def _():
            pass_on(0, z, head, True).start()

        @pl.when(z < n_head - 1)
        def _():
            pass_on(1, z, head, True).start()

    w_load.wait()

    def joined(source):
        return jnp.concatenate([source[head] for head in range(heads)], axis=1)

    total_out[...] = jnp.dot(joined(mine), w_buf[z], preferred_element_type=jnp.float32)
    shard_of = near_first(z, n_head)

    def gather_step(step, carry):
        shard = shard_of(step)
        for head in range(heads):

            @pl.when(shard > z)
            def _():
                pass_on(0, shard, head, False).wait_recv()

                @pl.when(z > 0)
                def _():
                    pass_on(0, shard, head, False).start()

            @pl.when(shard < z)
            def _():
                pass_on(1, shard, head, False).wait_recv()

                @pl.when(z < n_head - 1)
                def _():
                    pass_on(1, shard, head, False).start()

        total_out[...] += jnp.dot(
            joined(gbuf.at[shard]), w_buf[shard], preferred_element_type=jnp.float32
        )
        return carry

    lax.fori_loop(1, n_head, gather_step, 0)
    out[...] = total_out[...].astype(jnp.bfloat16)

    def drain_gather(step, carry):
        shard = shard_of(step)
        for head in range(heads):

            @pl.when((shard >= z) & (z > 0))
            def _():
                pass_on(0, shard, head, False).wait_send()

            @pl.when((shard <= z) & (z < n_head - 1))
            def _():
                pass_on(1, shard, head, False).wait_send()

        return carry

    lax.fori_loop(0, n_head, drain_gather, 0)

    def drain(step, carry):
        shards = (me - step, me + step)
        live = (me - step >= 0, me + step < size)
        for strand in range(2):

            @pl.when(live[strand] & passes_on[strand])
            def _():
                hop(strand, shards[strand], False).wait_send()

        return carry

    lax.fori_loop(0, size, drain, 0)


def vmem():
    return pl.BlockSpec(memory_space=pltpu.VMEM)


def anywhere():
    return pl.BlockSpec(memory_space=pl.ANY)


def shards(
    hidden,
    strand_bases,
    variant_sites,
    base_shift,
    base_embed,
    query_weight,
    key_weight,
    value_weight,
    out_weight,
):
    rows, feats = hidden.shape[1], hidden.shape[2]
    n_head = lax.axis_size("head")
    n_ctx = lax.axis_size("ctx")
    window = rows * n_ctx
    me = lax.axis_index("ctx")
    start = me * rows
    slots = 2 * VAR_DEV
    wide = rows + slots
    hw = query_weight.shape[1]
    heads = hw // HEAD_DIM
    width = query_weight.shape[0]

    z = lax.axis_index("head")
    n_plane = lax.axis_size("groups") * n_ctx
    part_rows = hw // n_plane
    plane = lax.axis_index("groups") * n_ctx + me
    w_part = lax.dynamic_slice_in_dim(out_weight, plane * part_rows, part_rows, 0)

    def w_block(owner):
        return lax.dynamic_slice_in_dim(w_part, owner * feats, feats, 1)

    w_mine = jnp.zeros((n_head, part_rows, feats), jnp.bfloat16)
    for shift in range(n_head):
        block = w_block(lax.rem(z + shift, n_head))
        if shift:
            block = lax.ppermute(
                block, "head", [(at, (at + shift) % n_head) for at in range(n_head)]
            )
        source = lax.rem(z - shift + n_head, n_head)
        w_mine = lax.dynamic_update_slice(w_mine, block[None], (source, 0, 0))
    w_all = lax.all_gather(w_mine, ("groups", "ctx"), axis=1, tiled=True)

    count = variant_sites.shape[0]
    order = jnp.arange(count, dtype=jnp.int32)
    row_iota = jnp.arange(rows, dtype=jnp.int32)
    v_block = variant_sites // rows
    before = (v_block[:, None] == v_block[None, :]) & (order[None, :] < order[:, None])
    rank = jnp.sum(before.astype(jnp.int32), axis=1)
    mine = v_block == me
    slot_iota = jnp.arange(slots, dtype=jnp.int32)
    slot_match = (rank[:, None] == slot_iota[None, :]) & mine[:, None]
    row_match = ((variant_sites - start)[:, None] == row_iota[None, :]) & mine[:, None]
    old_base = jnp.sum(jnp.where(row_match, strand_bases[None, :], 0), axis=1)
    new_base = jnp.mod(old_base + base_shift, 4)
    slot_old = jnp.sum(jnp.where(slot_match, old_base[:, None], 0), axis=0)
    slot_new = jnp.sum(jnp.where(slot_match, new_base[:, None], 0), axis=0)
    slot_live = jnp.any(slot_match, axis=0)
    has_row = jnp.any(row_match, axis=0).astype(jnp.float32)[:, None]

    all_slot = v_block * slots + rank
    all_match = all_slot[:, None] == jnp.arange(n_ctx * slots, dtype=jnp.int32)[None, :]
    all_pos = jnp.sum(jnp.where(all_match, variant_sites[:, None], 0), axis=0)
    all_live = jnp.any(all_match, axis=0)
    slot_pos = jnp.sum(jnp.where(slot_match, variant_sites[:, None], 0), axis=0)
    place = jnp.arange(window, dtype=jnp.int32)
    has_key = jnp.any(variant_sites[:, None] == place[None, :], axis=0)
    kt_mut = jnp.stack(
        [
            jnp.concatenate(
                [
                    jnp.where(has_key, FAR, flip(place)).reshape(n_ctx, rows),
                    jnp.where(all_live, flip(all_pos), FAR).reshape(n_ctx, slots),
                ],
                axis=1,
            )
            for flip in (lambda p: p, lambda p: window - 1 - p)
        ]
    )[:, :, None, :]

    sel = (
        (jnp.where(slot_live, slot_pos - start, -1)[:, None] == row_iota[None, :])
    ).astype(jnp.bfloat16)
    sel_t = (
        (row_iota[:, None] == jnp.where(slot_live, slot_pos - start, -1)[None, :])
    ).astype(jnp.bfloat16)
    code_iota = jnp.arange(4, dtype=jnp.int32)

    def signed(new, old):
        hot = (new[:, None] == code_iota[None, :]).astype(jnp.float32) - (
            old[:, None] == code_iota[None, :]
        ).astype(jnp.float32)
        return jnp.where(slot_live[:, None], hot, 0.0)

    codes = jnp.stack([signed(slot_new, slot_old), signed(3 - slot_new, 3 - slot_old)])
    table = base_embed.astype(jnp.float32)

    plus_pos = jnp.concatenate([start + row_iota, slot_pos])
    pos = jnp.stack([plus_pos, window - 1 - plus_pos]).astype(jnp.float32)
    half = HEAD_DIM // 2
    freq = jnp.power(ROPE_BASE, -jnp.arange(half, dtype=jnp.float32) * 2.0 / HEAD_DIM)
    angle = pos[:, :, None] * freq[None, None, :]
    cos_half, sin_half = jnp.cos(angle), jnp.sin(angle)
    cos = jnp.concatenate([cos_half, cos_half], axis=-1)
    sin = jnp.concatenate([-sin_half, sin_half], axis=-1)

    queries, cache = pl.pallas_call(
        functools.partial(project_kernel, n_head),
        out_shape=(
            jax.ShapeDtypeStruct((2, 2, rows, hw), jnp.bfloat16),
            jax.ShapeDtypeStruct((2, wide, 2 * hw), jnp.bfloat16),
        ),
        in_specs=[anywhere()] * 4 + [vmem()] * 7,
        out_specs=(vmem(), vmem()),
        scratch_shapes=[
            pltpu.VMEM((2, n_head, rows, feats), jnp.bfloat16),
            pltpu.VMEM((3, width, hw), jnp.bfloat16),
            pltpu.VMEM((wide, feats), jnp.bfloat16),
            pltpu.VMEM((wide, 3 * hw), jnp.float32),
            pltpu.SemaphoreType.DMA((2,)),
            pltpu.SemaphoreType.DMA((3,)),
            pltpu.SemaphoreType.DMA((2, 2, n_head, PIECES)),
            pltpu.SemaphoreType.DMA((2, n_head, PIECES)),
        ],
        compiler_params=pltpu.CompilerParams(
            collective_id=0, has_side_effects=True, vmem_limit_bytes=VMEM_LIMIT
        ),
        name="project",
    )(
        hidden,
        query_weight,
        key_weight,
        value_weight,
        sel,
        sel_t,
        has_row,
        codes,
        table,
        cos,
        sin,
    )

    return pl.pallas_call(
        functools.partial(attend_kernel, n_ctx, n_head),
        out_shape=jax.ShapeDtypeStruct((rows, feats), jnp.bfloat16),
        in_specs=[vmem()] * 3 + [anywhere()],
        out_specs=vmem(),
        scratch_shapes=[
            pltpu.VMEM((2, n_ctx, wide, 2 * hw), jnp.bfloat16),
            pltpu.VMEM((2, heads, 2, rows, 1), jnp.float32),
            pltpu.VMEM((2, heads, 2, rows, 1), jnp.float32),
            pltpu.VMEM((2, heads, 2, rows, HEAD_DIM), jnp.float32),
            pltpu.VMEM((n_head, hw, feats), jnp.bfloat16),
            pltpu.VMEM((n_head, heads, rows, HEAD_DIM), jnp.bfloat16),
            pltpu.VMEM((heads, rows, HEAD_DIM), jnp.bfloat16),
            pltpu.VMEM((rows, feats), jnp.float32),
            pltpu.SemaphoreType.DMA((2, n_ctx)),
            pltpu.SemaphoreType.DMA((2, n_ctx)),
            pltpu.SemaphoreType.DMA(()),
            pltpu.SemaphoreType.DMA((2, n_head, heads)),
            pltpu.SemaphoreType.DMA((n_head, heads)),
        ],
        compiler_params=pltpu.CompilerParams(
            collective_id=1, has_side_effects=True, vmem_limit_bytes=VMEM_LIMIT
        ),
        name="attend",
    )(queries, cache, kt_mut, w_all)


def solution(mesh):
    return jax.shard_map(
        shards,
        mesh=mesh,
        in_specs=(
            P(None, ("groups", "ctx"), "head"),
            P(("groups", "ctx")),
            P("groups"),
            P("groups"),
            P(),
            P(None, "head"),
            P(None, "head"),
            P(None, "head"),
            P("head", None),
        ),
        out_specs=P(("groups", "ctx"), "head"),
        check_vma=False,
    )
```

```python
import functools
import math

import jax
import jax.numpy as jnp
from jax import lax
from jax.experimental import pallas as pl
from jax.experimental.pallas import tpu as pltpu
from jax.sharding import PartitionSpec as P

HEAD_DIM = 128
VAR_DEV = 32
ROPE_BASE = 10000.0
NEG_FILL = -1e30
FAR = float(1 << 29)
PIECES = 2
MESH = pl.DeviceIdType.MESH
VMEM_LIMIT = 60 * 1024 * 1024


def greet(*axes):
    barrier = pltpu.get_barrier_semaphore()
    peers = 0
    for axis, size in axes:
        me = lax.axis_index(axis)

        @pl.when(me > 0)
        def _():
            pl.semaphore_signal(barrier, inc=1, device_id={axis: me - 1}, device_id_type=MESH)

        @pl.when(me < size - 1)
        def _():
            pl.semaphore_signal(barrier, inc=1, device_id={axis: me + 1}, device_id_type=MESH)

        peers = peers + jnp.minimum(me, 1) + jnp.minimum(size - 1 - me, 1)
    pl.semaphore_wait(barrier, peers)


def greet_all(axis, size):
    me = lax.axis_index(axis)
    barrier = pltpu.get_barrier_semaphore()
    for shift in range(1, size):
        pl.semaphore_signal(
            barrier, inc=1, device_id={axis: (me + shift) % size}, device_id_type=MESH
        )
    pl.semaphore_wait(barrier, size - 1)


def iota(shape, axis):
    return lax.broadcasted_iota(jnp.int32, shape, axis).astype(jnp.float32)


def to_column(row):
    size = row.shape[1]
    eye = iota((size, 1), 0) == iota((1, size), 1)
    return jnp.sum(jnp.where(eye, row, 0.0), axis=1, keepdims=True)


def slot_of(sites_row, sites_col, begin, rows):
    count = sites_row.shape[1]

    def inside(sites):
        return jnp.where((sites >= begin) & (sites < begin + rows), 1.0, 0.0)

    in_row, in_col = inside(sites_row), inside(sites_col)
    at_row, at_col = iota((1, count), 1), iota((count, 1), 0)
    rank_col = jnp.sum(jnp.where(at_row < at_col, in_row, 0.0), axis=1, keepdims=True)
    rank_row = jnp.sum(jnp.where(at_col < at_row, in_col, 0.0), axis=0, keepdims=True)
    return (
        jnp.where(in_row > 0.5, rank_row, -1.0),
        jnp.where(in_col > 0.5, rank_col, -1.0),
    )


def slot_row(slot_col, sites_col, slots):
    match = slot_col == iota((1, slots), 1)
    place = jnp.sum(jnp.where(match, sites_col, 0.0), axis=0, keepdims=True)
    live = jnp.sum(jnp.where(match, 1.0, 0.0), axis=0, keepdims=True)
    return place, live


def near_first(z, size):
    shorter = jnp.minimum(z, size - 1 - z)
    long_side = jnp.where(z < size - 1 - z, 1, -1)

    def shard_of(step):
        paired = jnp.where(step % 2 == 1, (step + 1) // 2, -((step + 1) // 2))
        return z + jnp.where(step <= 2 * shorter, paired, long_side * (step - shorter))

    return shard_of


class Layer:
    def __init__(self, size, slots, strand, hidden, weights, small, work, sems):
        self.size, self.slots, self.strand = size, slots, strand
        self.hidden, self.weights = hidden, weights
        self.sites, self.shift, self.bases, self.embed, self.freq = small
        self.xbuf, self.wbuf, self.stk, self.acc = work
        self.own_sem, self.w_sem, self.s_sem, self.r_sem = sems
        self.z = lax.axis_index("head")
        self.rows, self.feats = hidden.shape[1], hidden.shape[2]
        self.hw = weights[0].shape[1]
        self.piece = self.rows // PIECES
        self.shard_of = near_first(self.z, size)

    def hop(self, side, shard, part, own=False):
        span = pl.ds(part * self.piece, self.piece)
        return pltpu.make_async_remote_copy(
            src_ref=self.hidden.at[self.strand, span] if own else self.xbuf.at[shard, span],
            dst_ref=self.xbuf.at[shard, span],
            send_sem=self.s_sem.at[side, shard, part],
            recv_sem=self.r_sem.at[shard, part],
            device_id={"head": self.z - 1 if side == 0 else self.z + 1},
            device_id_type=MESH,
        )

    def open(self):
        z = self.z
        for part in range(PIECES):

            @pl.when(z > 0)
            def _():
                self.hop(0, z, part, True).start()

            @pl.when(z < self.size - 1)
            def _():
                self.hop(1, z, part, True).start()

    def load(self):
        copies = [
            pltpu.make_async_copy(
                self.hidden.at[self.strand], self.xbuf.at[self.z], self.own_sem
            )
        ] + [
            pltpu.make_async_copy(weight, self.wbuf.at[index], self.w_sem.at[index])
            for index, weight in enumerate(self.weights)
        ]
        for copy in copies:
            copy.start()
        return copies

    def tables(self):
        rows, slots = self.rows, self.slots
        me = lax.axis_index("ctx")
        begin = (me * rows).astype(jnp.float32)
        window = rows * lax.axis_size("ctx")
        sites_row = self.sites[...].astype(jnp.float32)
        sites_col = to_column(sites_row)
        slot_r, slot_c = slot_of(sites_row, sites_col, begin, rows)
        place_r, live_r = slot_row(slot_c, sites_col, slots)
        match_t = iota((slots, 1), 0) == slot_r
        place_c = jnp.sum(jnp.where(match_t, sites_row, 0.0), axis=1, keepdims=True)
        self.live = jnp.sum(jnp.where(match_t, 1.0, 0.0), axis=1, keepdims=True)
        shift = jnp.sum(
            jnp.where(match_t, self.shift[...].astype(jnp.float32), 0.0), axis=1, keepdims=True
        )
        local_c = jnp.where(self.live > 0.5, place_c - begin, -1.0)
        local_r = jnp.where(live_r > 0.5, place_r - begin, -1.0)
        hit = local_c == iota((1, rows), 1)
        hit_t = iota((rows, 1), 0) == local_r
        self.sel = jnp.where(hit, 1.0, 0.0).astype(jnp.bfloat16)
        spread = jnp.where(hit_t, 1.0, 0.0)
        self.sel_t = spread.astype(jnp.bfloat16)
        self.has_row = jnp.sum(spread, axis=1, keepdims=True)
        old = jnp.sum(
            jnp.where(hit, self.bases[...].astype(jnp.float32), 0.0), axis=1, keepdims=True
        )
        new = old + shift
        new = jnp.where(new >= 4.0, new - 4.0, new)
        if self.strand == 1:
            old, new = 3.0 - old, 3.0 - new
        self.coefs = [
            jnp.where(
                self.live > 0.5,
                jnp.where(new == code, 1.0, 0.0) - jnp.where(old == code, 1.0, 0.0),
                0.0,
            )
            for code in range(4)
        ]
        place = jnp.concatenate([begin + iota((rows, 1), 0), place_c], axis=0)
        if self.strand == 1:
            place = window - 1 - place
        angle = place * self.freq[...]
        self.cos = jnp.cos(angle)
        side = jnp.where(iota((1, HEAD_DIM), 1) < HEAD_DIM // 2, -1.0, 1.0)
        self.sin = jnp.sin(angle) * side

    def run(self, between=None):
        z, size, rows, feats, hw = self.z, self.size, self.rows, self.feats, self.hw
        self.acc[...] = jnp.zeros_like(self.acc)

        def step_body(step, carry):
            shard = self.shard_of(step)
            for part in range(PIECES):

                @pl.when(shard > z)
                def _():
                    self.hop(0, shard, part).wait_recv()

                    @pl.when(z > 0)
                    def _():
                        self.hop(0, shard, part).start()

                @pl.when(shard < z)
                def _():
                    self.hop(1, shard, part).wait_recv()

                    @pl.when(z < size - 1)
                    def _():
                        self.hop(1, shard, part).start()

            block = self.xbuf[shard]
            self.stk[pl.ds(0, rows), :] = block
            first = pl.multiple_of(shard * feats, feats)
            letters = self.embed[:, pl.ds(first, feats)].astype(jnp.float32)
            diff = sum(self.coefs[code] * letters[code : code + 1] for code in range(4))
            picked = jnp.dot(self.sel, block, preferred_element_type=jnp.float32)
            self.stk[pl.ds(rows, self.slots), :] = (picked + diff).astype(jnp.bfloat16)
            for index in range(3):
                self.acc[:, pl.ds(index * hw, hw)] += jnp.dot(
                    self.stk[...],
                    self.wbuf[index, pl.ds(first, feats), :],
                    preferred_element_type=jnp.float32,
                )
            if between is not None:
                between(step)
            return carry

        lax.fori_loop(0, size, step_body, 0)

    def finish(self, q_out, kv_out):
        rows, hw = self.rows, self.hw
        for head in range(hw // HEAD_DIM):
            cols = pl.ds(head * HEAD_DIM, HEAD_DIM)
            for index in range(2):
                raw = self.acc[:, pl.ds(index * hw + head * HEAD_DIM, HEAD_DIM)]
                turned = raw * self.cos + pltpu.roll(raw, HEAD_DIM // 2, 1) * self.sin
                turned = turned.astype(jnp.bfloat16)
                if index == 0:
                    base = turned[:rows]
                    placed = jnp.dot(
                        self.sel_t, turned[rows:], preferred_element_type=jnp.float32
                    )
                    q_out[0, :, cols] = base
                    q_out[1, :, cols] = jnp.where(
                        self.has_row > 0.5, placed, base.astype(jnp.float32)
                    ).astype(jnp.bfloat16)
                else:
                    kv_out[:, cols] = turned
        kv_out[:, pl.ds(hw, hw)] = self.acc[:, pl.ds(2 * hw, hw)].astype(jnp.bfloat16)

    def drain(self):
        z = self.z

        def body(step, carry):
            shard = self.shard_of(step)
            for part in range(PIECES):

                @pl.when((shard >= z) & (z > 0))
                def _():
                    self.hop(0, shard, part).wait_send()

                @pl.when((shard <= z) & (z < self.size - 1))
                def _():
                    self.hop(1, shard, part).wait_send()

            return carry

        lax.fori_loop(0, self.size, body, 0)


class Attention:
    def __init__(self, size, slots, strand, q_in, kv_in, sites, work):
        self.size, self.slots, self.strand = size, slots, strand
        self.q_in, self.kv_in = q_in, kv_in
        self.kvbuf, self.m_buf, self.l_buf, self.a_buf, self.s_sem, self.r_sem = work
        self.me = lax.axis_index("ctx")
        self.rows, self.hw = q_in.shape[1], q_in.shape[2]
        self.heads = self.hw // HEAD_DIM
        self.window = self.rows * size
        self.passes_on = self.me < size - 1 if strand == 0 else self.me > 0
        self.sites_row = sites[...].astype(jnp.float32)
        self.sites_col = to_column(self.sites_row)

    def hop(self, shard, own=False):
        return pltpu.make_async_remote_copy(
            src_ref=self.kv_in if own else self.kvbuf.at[shard],
            dst_ref=self.kvbuf.at[shard],
            send_sem=self.s_sem.at[shard],
            recv_sem=self.r_sem.at[shard],
            device_id={"ctx": self.me + 1 if self.strand == 0 else self.me - 1},
            device_id_type=MESH,
        )

    def open(self):
        @pl.when(self.passes_on)
        def _():
            self.hop(self.me, True).start()

    def clock(self, place):
        return place if self.strand == 0 else self.window - 1 - place

    def update(self, shard, block, first):
        rows, hw, slots = self.rows, self.hw, self.slots
        q_time = self.clock((self.me * rows).astype(jnp.float32) + iota((rows, 1), 0))
        begin = (shard * rows).astype(jnp.float32)
        place = begin + iota((1, rows), 1)
        ref_time = self.clock(place)
        _, slot_c = slot_of(self.sites_row, self.sites_col, begin, rows)
        slot_place, live = slot_row(slot_c, self.sites_col, slots)
        taken = jnp.sum(jnp.where(self.sites_col == place, 1.0, 0.0), axis=0, keepdims=True)
        mut_time = jnp.concatenate(
            [
                jnp.where(taken > 0.5, FAR, ref_time),
                jnp.where(live > 0.5, self.clock(slot_place), FAR),
            ],
            axis=1,
        )
        k_times = (ref_time, mut_time)
        spans = (rows, rows + slots)
        log_scale = math.log2(math.e) / math.sqrt(HEAD_DIM)

        def one_head(head, carry):
            k_cols = pl.ds(pl.multiple_of(head * HEAD_DIM, HEAD_DIM), HEAD_DIM)
            v_cols = pl.ds(pl.multiple_of(hw + head * HEAD_DIM, HEAD_DIM), HEAD_DIM)
            for kind in range(2):
                span = pl.ds(0, spans[kind])
                raw = lax.dot_general(
                    self.q_in[kind, :, k_cols],
                    block[span, k_cols],
                    (((1,), (1,)), ((), ())),
                    preferred_element_type=jnp.float32,
                )
                raw = jnp.where(k_times[kind] <= q_time, raw, NEG_FILL)
                top = jnp.max(raw, axis=1, keepdims=True)
                if not first:
                    old = self.m_buf[head, kind]
                    top = jnp.maximum(old, top)
                    fade = jnp.exp2((old - top) * log_scale)
                weights = jnp.exp2((raw - top) * log_scale)
                total = jnp.sum(weights, axis=1, keepdims=True)
                vec = jnp.dot(
                    weights.astype(jnp.bfloat16),
                    block[span, v_cols],
                    preferred_element_type=jnp.float32,
                )
                if not first:
                    total = total + fade * self.l_buf[head, kind]
                    vec = vec + fade * self.a_buf[head, kind]
                self.m_buf[head, kind] = top
                self.l_buf[head, kind] = total
                self.a_buf[head, kind] = vec
            return carry

        lax.fori_loop(0, self.heads, one_head, 0)

    def own_block(self):
        self.update(self.me, self.kv_in, True)

    def shard_at(self, step):
        return self.me - step if self.strand == 0 else self.me + step

    def alive(self, step):
        shard = self.shard_at(step)
        return shard >= 0 if self.strand == 0 else shard < self.size

    def arrive(self, step):
        shard = self.shard_at(step)

        @pl.when(self.alive(step))
        def _():
            self.hop(shard).wait_recv()

            @pl.when(self.passes_on)
            def _():
                self.hop(shard).start()

            self.update(shard, self.kvbuf.at[shard], False)

    def change(self, head):
        return self.a_buf[head, 0] / self.l_buf[head, 0] - self.a_buf[head, 1] / self.l_buf[head, 1]

    def drain(self):
        def body(step, carry):
            @pl.when(self.alive(step) & self.passes_on)
            def _():
                self.hop(self.shard_at(step)).wait_send()

            return carry

        lax.fori_loop(0, self.size, body, 0)


def plus_kernel(
    n_head,
    slots,
    hidden,
    wq,
    wk,
    wv,
    out_w,
    sites,
    shift,
    bases,
    embed,
    freq,
    q_out,
    kv_out,
    w_out,
    *rest,
):
    work, sems, (x_send, x_recv, x_own) = rest[:4], rest[4:8], rest[8:]
    z = lax.axis_index("head")
    plane = lax.axis_index("groups") * lax.axis_size("ctx") + lax.axis_index("ctx")
    part, feats = w_out.shape[1], w_out.shape[2]
    part_rows = pl.ds(pl.multiple_of(plane * part, part), part)
    greet_all("head", n_head)
    layer = Layer(
        n_head, slots, 0, hidden, (wq, wk, wv), (sites, shift, bases, embed, freq), work, sems
    )
    layer.open()

    def trade(shift):
        owner = (z + shift) % n_head
        cols = pl.ds(pl.multiple_of(owner * feats, feats), feats)
        return pltpu.make_async_remote_copy(
            src_ref=out_w.at[part_rows, cols],
            dst_ref=w_out.at[z],
            send_sem=x_send.at[owner],
            recv_sem=x_recv.at[z],
            device_id={"head": owner},
            device_id_type=MESH,
        )

    def traded(shift):
        source = (z + shift) % n_head
        cols = pl.ds(pl.multiple_of(z * feats, feats), feats)
        return pltpu.make_async_remote_copy(
            src_ref=out_w.at[part_rows, cols],
            dst_ref=w_out.at[source],
            send_sem=x_send.at[source],
            recv_sem=x_recv.at[source],
            device_id={"head": source},
            device_id_type=MESH,
        )

    for step in range(1, n_head):
        trade(step).start()
    keep = pltpu.make_async_copy(
        out_w.at[part_rows, pl.ds(pl.multiple_of(z * feats, feats), feats)], w_out.at[z], x_own
    )
    loads = layer.load() + [keep]
    keep.start()
    layer.tables()
    for copy in loads:
        copy.wait()
    layer.run()
    layer.finish(q_out, kv_out)
    for step in range(1, n_head):
        traded(step).wait_recv()
        trade(step).wait_send()
    layer.drain()


def minus_kernel(
    n_head,
    n_ctx,
    slots,
    hidden,
    wq,
    wk,
    wv,
    sites,
    shift,
    bases,
    embed,
    freq,
    q_plus,
    kv_plus,
    q_out,
    kv_out,
    change,
    *rest,
):
    work, sems, seen = rest[:4], rest[4:8], rest[8:]
    greet(("head", n_head), ("ctx", n_ctx))
    layer = Layer(
        n_head, slots, 1, hidden, (wq, wk, wv), (sites, shift, bases, embed, freq), work, sems
    )
    attention = Attention(n_ctx, slots, 0, q_plus, kv_plus, sites, seen)
    layer.open()
    attention.open()
    loads = layer.load()
    layer.tables()
    attention.own_block()
    for copy in loads:
        copy.wait()

    def between(step):
        span = max(n_head - 2, 1)
        low = 1 + jnp.maximum(step - 1, 0) * (n_ctx - 1) // span
        high = 1 + step * (n_ctx - 1) // span
        high = jnp.minimum(high, n_ctx)

        def body(at, carry):
            attention.arrive(at)
            return carry

        lax.fori_loop(low, high, body, 0)

    layer.run(between)
    layer.finish(q_out, kv_out)
    for head in range(attention.heads):
        change[head] = attention.change(head)
    attention.drain()
    layer.drain()


def last_kernel(
    n_head,
    n_ctx,
    slots,
    q_in,
    kv_in,
    sites,
    change,
    w_in,
    out,
    w_buf,
    gbuf,
    mine,
    total_out,
    w_sem,
    gs_sem,
    gr_sem,
    *seen,
):
    z = lax.axis_index("head")
    greet(("ctx", n_ctx), ("head", n_head))
    attention = Attention(n_ctx, slots, 1, q_in, kv_in, sites, seen)
    heads = attention.heads
    attention.open()
    w_load = pltpu.make_async_copy(w_in, w_buf, w_sem)
    w_load.start()
    attention.own_block()

    def body(at, carry):
        attention.arrive(at)
        return carry

    lax.fori_loop(1, n_ctx, body, 0)

    def pass_on(side, shard, head, own):
        return pltpu.make_async_remote_copy(
            src_ref=mine.at[head] if own else gbuf.at[shard, head],
            dst_ref=gbuf.at[shard, head],
            send_sem=gs_sem.at[side, shard, head],
            recv_sem=gr_sem.at[shard, head],
            device_id={"head": z - 1 if side == 0 else z + 1},
            device_id_type=MESH,
        )

    for head in range(heads):
        mine[head] = (0.5 * (change[head] + attention.change(head))).astype(jnp.bfloat16)

        @pl.when(z > 0)
        def _():
            pass_on(0, z, head, True).start()

        @pl.when(z < n_head - 1)
        def _():
            pass_on(1, z, head, True).start()

    w_load.wait()

    def joined(source):
        return jnp.concatenate([source[head] for head in range(heads)], axis=1)

    total_out[...] = jnp.dot(joined(mine), w_buf[z], preferred_element_type=jnp.float32)
    shard_of = near_first(z, n_head)

    def gather_step(step, carry):
        shard = shard_of(step)
        for head in range(heads):

            @pl.when(shard > z)
            def _():
                pass_on(0, shard, head, False).wait_recv()

                @pl.when(z > 0)
                def _():
                    pass_on(0, shard, head, False).start()

            @pl.when(shard < z)
            def _():
                pass_on(1, shard, head, False).wait_recv()

                @pl.when(z < n_head - 1)
                def _():
                    pass_on(1, shard, head, False).start()

        total_out[...] += jnp.dot(
            joined(gbuf.at[shard]), w_buf[shard], preferred_element_type=jnp.float32
        )
        return carry

    lax.fori_loop(1, n_head, gather_step, 0)
    out[...] = total_out[...].astype(jnp.bfloat16)

    def drain_gather(step, carry):
        shard = shard_of(step)
        for head in range(heads):

            @pl.when((shard >= z) & (z > 0))
            def _():
                pass_on(0, shard, head, False).wait_send()

            @pl.when((shard <= z) & (z < n_head - 1))
            def _():
                pass_on(1, shard, head, False).wait_send()

        return carry

    lax.fori_loop(0, n_head, drain_gather, 0)
    attention.drain()


def vmem():
    return pl.BlockSpec(memory_space=pltpu.VMEM)


def anywhere():
    return pl.BlockSpec(memory_space=pl.ANY)


def shards(
    hidden,
    strand_bases,
    variant_sites,
    base_shift,
    base_embed,
    query_weight,
    key_weight,
    value_weight,
    out_weight,
):
    rows, feats = hidden.shape[1], hidden.shape[2]
    n_head = lax.axis_size("head")
    n_ctx = lax.axis_size("ctx")
    slots = 2 * VAR_DEV
    wide = rows + slots
    width, hw = query_weight.shape
    heads = hw // HEAD_DIM
    part = hw // (lax.axis_size("groups") * n_ctx)

    half = HEAD_DIM // 2
    freq = jnp.power(ROPE_BASE, -jnp.arange(half, dtype=jnp.float32) * 2.0 / HEAD_DIM)
    small = (
        variant_sites[None, :],
        base_shift[None, :],
        strand_bases[None, :],
        base_embed,
        jnp.concatenate([freq, freq])[None, :],
    )
    weights = (query_weight, key_weight, value_weight)
    layer_work = [
        pltpu.VMEM((n_head, rows, feats), jnp.bfloat16),
        pltpu.VMEM((3, width, hw), jnp.bfloat16),
        pltpu.VMEM((wide, feats), jnp.bfloat16),
        pltpu.VMEM((wide, 3 * hw), jnp.float32),
        pltpu.SemaphoreType.DMA(()),
        pltpu.SemaphoreType.DMA((3,)),
        pltpu.SemaphoreType.DMA((2, n_head, PIECES)),
        pltpu.SemaphoreType.DMA((n_head, PIECES)),
    ]
    attend_work = [
        pltpu.VMEM((n_ctx, wide, 2 * hw), jnp.bfloat16),
        pltpu.VMEM((heads, 2, rows, 1), jnp.float32),
        pltpu.VMEM((heads, 2, rows, 1), jnp.float32),
        pltpu.VMEM((heads, 2, rows, HEAD_DIM), jnp.float32),
        pltpu.SemaphoreType.DMA((n_ctx,)),
        pltpu.SemaphoreType.DMA((n_ctx,)),
    ]
    q_shape = jax.ShapeDtypeStruct((2, rows, hw), jnp.bfloat16)
    kv_shape = jax.ShapeDtypeStruct((wide, 2 * hw), jnp.bfloat16)

    def call(kernel, number, out_shape, in_specs, scratch, name):
        return pl.pallas_call(
            kernel,
            out_shape=out_shape,
            in_specs=in_specs,
            out_specs=jax.tree.map(lambda _: vmem(), out_shape),
            scratch_shapes=scratch,
            compiler_params=pltpu.CompilerParams(
                collective_id=number, has_side_effects=True, vmem_limit_bytes=VMEM_LIMIT
            ),
            name=name,
        )

    q_plus, kv_plus, w_mine = call(
        functools.partial(plus_kernel, n_head, slots),
        0,
        (q_shape, kv_shape, jax.ShapeDtypeStruct((n_head, part, feats), jnp.bfloat16)),
        [anywhere()] * 5 + [vmem()] * 5,
        layer_work
        + [
            pltpu.SemaphoreType.DMA((n_head,)),
            pltpu.SemaphoreType.DMA((n_head,)),
            pltpu.SemaphoreType.DMA(()),
        ],
        "project_plus",
    )(hidden, *weights, out_weight, *small)
    w_all = lax.all_gather(w_mine, ("groups", "ctx"), axis=1, tiled=True)
    q_minus, kv_minus, change = call(
        functools.partial(minus_kernel, n_head, n_ctx, slots),
        1,
        (q_shape, kv_shape, jax.ShapeDtypeStruct((heads, rows, HEAD_DIM), jnp.float32)),
        [anywhere()] * 4 + [vmem()] * 7,
        layer_work + attend_work,
        "attend_plus",
    )(hidden, *weights, *small, q_plus, kv_plus)
    return call(
        functools.partial(last_kernel, n_head, n_ctx, slots),
        2,
        jax.ShapeDtypeStruct((rows, feats), jnp.bfloat16),
        [vmem()] * 4 + [anywhere()],
        [
            pltpu.VMEM((n_head, hw, feats), jnp.bfloat16),
            pltpu.VMEM((n_head, heads, rows, HEAD_DIM), jnp.bfloat16),
            pltpu.VMEM((heads, rows, HEAD_DIM), jnp.bfloat16),
            pltpu.VMEM((rows, feats), jnp.float32),
            pltpu.SemaphoreType.DMA(()),
            pltpu.SemaphoreType.DMA((2, n_head, heads)),
            pltpu.SemaphoreType.DMA((n_head, heads)),
        ]
        + attend_work,
        "attend_minus",
    )(q_minus, kv_minus, small[0], change, w_all)


def solution(mesh):
    return jax.shard_map(
        shards,
        mesh=mesh,
        in_specs=(
            P(None, ("groups", "ctx"), "head"),
            P(("groups", "ctx")),
            P("groups"),
            P("groups"),
            P(),
            P(None, "head"),
            P(None, "head"),
            P(None, "head"),
            P("head", None),
        ),
        out_specs=P(("groups", "ctx"), "head"),
        check_vma=False,
    )
```

```python
import functools
import math

import jax
import jax.numpy as jnp
from jax import lax
from jax.experimental import pallas as pl
from jax.experimental.pallas import tpu as pltpu
from jax.sharding import PartitionSpec as P

HEAD_DIM = 128
VAR_DEV = 32
ROPE_BASE = 10000.0
NEG_FILL = -1e30
FAR = float(1 << 29)
PIECES = 2
MESH = pl.DeviceIdType.MESH
VMEM_LIMIT = 60 * 1024 * 1024


def greet(*axes, all_of=None):
    barrier = pltpu.get_barrier_semaphore()
    peers = 0
    for axis, size in axes:
        me = lax.axis_index(axis)

        @pl.when(me > 0)
        def _():
            pl.semaphore_signal(barrier, inc=1, device_id={axis: me - 1}, device_id_type=MESH)

        @pl.when(me < size - 1)
        def _():
            pl.semaphore_signal(barrier, inc=1, device_id={axis: me + 1}, device_id_type=MESH)

        peers = peers + jnp.minimum(me, 1) + jnp.minimum(size - 1 - me, 1)
    if all_of is not None:
        axis, size = all_of
        me = lax.axis_index(axis)
        for shift in range(1, size):
            pl.semaphore_signal(
                barrier, inc=1, device_id={axis: (me + shift) % size}, device_id_type=MESH
            )
        peers = peers + size - 1
    pl.semaphore_wait(barrier, peers)


def greet_all(axis, size):
    me = lax.axis_index(axis)
    barrier = pltpu.get_barrier_semaphore()
    for shift in range(1, size):
        pl.semaphore_signal(
            barrier, inc=1, device_id={axis: (me + shift) % size}, device_id_type=MESH
        )
    pl.semaphore_wait(barrier, size - 1)


def iota(shape, axis):
    return lax.broadcasted_iota(jnp.int32, shape, axis).astype(jnp.float32)


def to_column(row):
    size = row.shape[1]
    eye = iota((size, 1), 0) == iota((1, size), 1)
    return jnp.sum(jnp.where(eye, row, 0.0), axis=1, keepdims=True)


def slot_of(sites_row, sites_col, begin, rows):
    count = sites_row.shape[1]

    def inside(sites):
        return jnp.where((sites >= begin) & (sites < begin + rows), 1.0, 0.0)

    in_row, in_col = inside(sites_row), inside(sites_col)
    at_row, at_col = iota((1, count), 1), iota((count, 1), 0)
    rank_col = jnp.sum(jnp.where(at_row < at_col, in_row, 0.0), axis=1, keepdims=True)
    rank_row = jnp.sum(jnp.where(at_col < at_row, in_col, 0.0), axis=0, keepdims=True)
    return (
        jnp.where(in_row > 0.5, rank_row, -1.0),
        jnp.where(in_col > 0.5, rank_col, -1.0),
    )


def slot_row(slot_col, sites_col, slots):
    match = slot_col == iota((1, slots), 1)
    place = jnp.sum(jnp.where(match, sites_col, 0.0), axis=0, keepdims=True)
    live = jnp.sum(jnp.where(match, 1.0, 0.0), axis=0, keepdims=True)
    return place, live


def near_first(z, size):
    shorter = jnp.minimum(z, size - 1 - z)
    long_side = jnp.where(z < size - 1 - z, 1, -1)

    def shard_of(step):
        paired = jnp.where(step % 2 == 1, (step + 1) // 2, -((step + 1) // 2))
        return z + jnp.where(step <= 2 * shorter, paired, long_side * (step - shorter))

    return shard_of


class Layer:
    def __init__(self, size, slots, strand, hidden, weights, small, work, sems):
        self.size, self.slots, self.strand = size, slots, strand
        self.hidden, self.weights = hidden, weights
        self.sites, self.shift, self.bases, self.embed, self.freq = small
        self.xbuf, self.wbuf, self.stk, self.acc = work
        self.own_sem, self.w_sem, self.s_sem, self.r_sem = sems
        self.z = lax.axis_index("head")
        self.rows, self.feats = hidden.shape[1], hidden.shape[2]
        self.hw = weights[0].shape[1]
        self.piece = self.rows // PIECES
        self.shard_of = near_first(self.z, size)

    def hop(self, side, shard, part, own=False):
        span = pl.ds(part * self.piece, self.piece)
        return pltpu.make_async_remote_copy(
            src_ref=self.hidden.at[self.strand, span] if own else self.xbuf.at[shard, span],
            dst_ref=self.xbuf.at[shard, span],
            send_sem=self.s_sem.at[side, shard, part],
            recv_sem=self.r_sem.at[shard, part],
            device_id={"head": self.z - 1 if side == 0 else self.z + 1},
            device_id_type=MESH,
        )

    def open(self):
        z = self.z
        for part in range(PIECES):

            @pl.when(z > 0)
            def _():
                self.hop(0, z, part, True).start()

            @pl.when(z < self.size - 1)
            def _():
                self.hop(1, z, part, True).start()

    def load(self):
        copies = [
            pltpu.make_async_copy(
                self.hidden.at[self.strand], self.xbuf.at[self.z], self.own_sem
            )
        ] + [
            pltpu.make_async_copy(weight, self.wbuf.at[index], self.w_sem.at[index])
            for index, weight in enumerate(self.weights)
        ]
        for copy in copies:
            copy.start()
        return copies

    def tables(self):
        rows, slots = self.rows, self.slots
        me = lax.axis_index("ctx")
        begin = (me * rows).astype(jnp.float32)
        window = rows * lax.axis_size("ctx")
        sites_row = self.sites[...].astype(jnp.float32)
        sites_col = to_column(sites_row)
        slot_r, slot_c = slot_of(sites_row, sites_col, begin, rows)
        place_r, live_r = slot_row(slot_c, sites_col, slots)
        match_t = iota((slots, 1), 0) == slot_r
        place_c = jnp.sum(jnp.where(match_t, sites_row, 0.0), axis=1, keepdims=True)
        self.live = jnp.sum(jnp.where(match_t, 1.0, 0.0), axis=1, keepdims=True)
        shift = jnp.sum(
            jnp.where(match_t, self.shift[...].astype(jnp.float32), 0.0), axis=1, keepdims=True
        )
        local_c = jnp.where(self.live > 0.5, place_c - begin, -1.0)
        local_r = jnp.where(live_r > 0.5, place_r - begin, -1.0)
        hit = local_c == iota((1, rows), 1)
        hit_t = iota((rows, 1), 0) == local_r
        self.sel = jnp.where(hit, 1.0, 0.0).astype(jnp.bfloat16)
        spread = jnp.where(hit_t, 1.0, 0.0)
        self.sel_t = spread.astype(jnp.bfloat16)
        self.has_row = jnp.sum(spread, axis=1, keepdims=True)
        old = jnp.sum(
            jnp.where(hit, self.bases[...].astype(jnp.float32), 0.0), axis=1, keepdims=True
        )
        new = old + shift
        new = jnp.where(new >= 4.0, new - 4.0, new)
        if self.strand == 1:
            old, new = 3.0 - old, 3.0 - new
        self.coefs = [
            jnp.where(
                self.live > 0.5,
                jnp.where(new == code, 1.0, 0.0) - jnp.where(old == code, 1.0, 0.0),
                0.0,
            )
            for code in range(4)
        ]
        place = jnp.concatenate([begin + iota((rows, 1), 0), place_c], axis=0)
        if self.strand == 1:
            place = window - 1 - place
        angle = place * self.freq[...]
        self.cos = jnp.cos(angle)
        side = jnp.where(iota((1, HEAD_DIM), 1) < HEAD_DIM // 2, -1.0, 1.0)
        self.sin = jnp.sin(angle) * side

    def run(self, between=None):
        z, size, rows, feats, hw = self.z, self.size, self.rows, self.feats, self.hw
        self.acc[...] = jnp.zeros_like(self.acc)

        def step_body(step, carry):
            shard = self.shard_of(step)
            for part in range(PIECES):

                @pl.when(shard > z)
                def _():
                    self.hop(0, shard, part).wait_recv()

                    @pl.when(z > 0)
                    def _():
                        self.hop(0, shard, part).start()

                @pl.when(shard < z)
                def _():
                    self.hop(1, shard, part).wait_recv()

                    @pl.when(z < size - 1)
                    def _():
                        self.hop(1, shard, part).start()

            block = self.xbuf[shard]
            self.stk[pl.ds(0, rows), :] = block
            first = pl.multiple_of(shard * feats, feats)
            letters = self.embed[:, pl.ds(first, feats)].astype(jnp.float32)
            diff = sum(self.coefs[code] * letters[code : code + 1] for code in range(4))
            picked = jnp.dot(self.sel, block, preferred_element_type=jnp.float32)
            self.stk[pl.ds(rows, self.slots), :] = (picked + diff).astype(jnp.bfloat16)
            for index in range(3):
                self.acc[:, pl.ds(index * hw, hw)] += jnp.dot(
                    self.stk[...],
                    self.wbuf[index, pl.ds(first, feats), :],
                    preferred_element_type=jnp.float32,
                )
            if between is not None:
                between(step)
            return carry

        lax.fori_loop(0, size, step_body, 0)

    def finish(self, q_out, kv_out):
        rows, hw = self.rows, self.hw
        for head in range(hw // HEAD_DIM):
            cols = pl.ds(head * HEAD_DIM, HEAD_DIM)
            for index in range(2):
                raw = self.acc[:, pl.ds(index * hw + head * HEAD_DIM, HEAD_DIM)]
                turned = raw * self.cos + pltpu.roll(raw, HEAD_DIM // 2, 1) * self.sin
                turned = turned.astype(jnp.bfloat16)
                if index == 0:
                    base = turned[:rows]
                    placed = jnp.dot(
                        self.sel_t, turned[rows:], preferred_element_type=jnp.float32
                    )
                    q_out[0, :, cols] = base
                    q_out[1, :, cols] = jnp.where(
                        self.has_row > 0.5, placed, base.astype(jnp.float32)
                    ).astype(jnp.bfloat16)
                else:
                    kv_out[head, :, pl.ds(0, HEAD_DIM)] = turned
            kv_out[head, :, pl.ds(HEAD_DIM, HEAD_DIM)] = self.acc[
                :, pl.ds(2 * hw + head * HEAD_DIM, HEAD_DIM)
            ].astype(jnp.bfloat16)

    def drain(self):
        z = self.z

        def body(step, carry):
            shard = self.shard_of(step)
            for part in range(PIECES):

                @pl.when((shard >= z) & (z > 0))
                def _():
                    self.hop(0, shard, part).wait_send()

                @pl.when((shard <= z) & (z < self.size - 1))
                def _():
                    self.hop(1, shard, part).wait_send()

            return carry

        lax.fori_loop(0, self.size, body, 0)


class Attention:
    def __init__(self, size, slots, strand, q_in, kv_in, sites, work):
        self.size, self.slots, self.strand = size, slots, strand
        self.q_in, self.kv_in = q_in, kv_in
        self.kvbuf, self.kt_buf, self.m_buf, self.l_buf, self.a_buf = work[:5]
        self.s_sem, self.r_sem = work[5:]
        self.me = lax.axis_index("ctx")
        self.rows, self.hw = q_in.shape[1], q_in.shape[2]
        self.heads = self.hw // HEAD_DIM
        self.window = self.rows * size
        self.passes_on = self.me < size - 1 if strand == 0 else self.me > 0
        self.sites_row = sites[...].astype(jnp.float32)
        self.sites_col = to_column(self.sites_row)

    def hop(self, shard, head, own=False):
        return pltpu.make_async_remote_copy(
            src_ref=self.kv_in.at[head] if own else self.kvbuf.at[shard, head],
            dst_ref=self.kvbuf.at[shard, head],
            send_sem=self.s_sem.at[shard, head],
            recv_sem=self.r_sem.at[shard, head],
            device_id={"ctx": self.me + 1 if self.strand == 0 else self.me - 1},
            device_id_type=MESH,
        )

    def open(self, head):
        @pl.when(self.passes_on & (head < self.heads))
        def _():
            self.hop(self.me, head, True).start()

    def clock(self, place):
        return place if self.strand == 0 else self.window - 1 - place

    def times(self):
        rows, slots = self.rows, self.slots

        def body(shard, carry):
            begin = (shard * rows).astype(jnp.float32)
            place = begin + iota((1, rows), 1)
            _, slot_c = slot_of(self.sites_row, self.sites_col, begin, rows)
            slot_place, live = slot_row(slot_c, self.sites_col, slots)
            taken = jnp.sum(
                jnp.where(self.sites_col == place, 1.0, 0.0), axis=0, keepdims=True
            )
            self.kt_buf[shard] = jnp.concatenate(
                [
                    jnp.where(taken > 0.5, FAR, self.clock(place)),
                    jnp.where(live > 0.5, self.clock(slot_place), FAR),
                ],
                axis=1,
            )
            return carry

        lax.fori_loop(0, self.size, body, 0)

    def update(self, shard, head, block, first):
        rows, slots = self.rows, self.slots
        q_time = self.clock((self.me * rows).astype(jnp.float32) + iota((rows, 1), 0))
        ref_time = self.clock((shard * rows).astype(jnp.float32) + iota((1, rows), 1))
        k_times = (ref_time, self.kt_buf[shard])
        spans = (rows, rows + slots)
        log_scale = math.log2(math.e) / math.sqrt(HEAD_DIM)
        cols = pl.ds(pl.multiple_of(head * HEAD_DIM, HEAD_DIM), HEAD_DIM)
        for kind in range(2):
            span = pl.ds(0, spans[kind])
            raw = lax.dot_general(
                self.q_in[kind, :, cols],
                block[span, pl.ds(0, HEAD_DIM)],
                (((1,), (1,)), ((), ())),
                preferred_element_type=jnp.float32,
            )
            raw = jnp.where(k_times[kind] <= q_time, raw, NEG_FILL)
            top = jnp.max(raw, axis=1, keepdims=True)
            if not first:
                old = self.m_buf[head, kind]
                top = jnp.maximum(old, top)
                fade = jnp.exp2((old - top) * log_scale)
            weights = jnp.exp2((raw - top) * log_scale)
            total = jnp.sum(weights, axis=1, keepdims=True)
            vec = jnp.dot(
                weights.astype(jnp.bfloat16),
                block[span, pl.ds(HEAD_DIM, HEAD_DIM)],
                preferred_element_type=jnp.float32,
            )
            if not first:
                total = total + fade * self.l_buf[head, kind]
                vec = vec + fade * self.a_buf[head, kind]
            self.m_buf[head, kind] = top
            self.l_buf[head, kind] = total
            self.a_buf[head, kind] = vec

    def own_block(self, head):
        self.update(self.me, head, self.kv_in.at[head], True)

    def shard_at(self, step):
        return self.me - step if self.strand == 0 else self.me + step

    def alive(self, step):
        shard = self.shard_at(step)
        return shard >= 0 if self.strand == 0 else shard < self.size

    def arrive(self, step, head):
        shard = self.shard_at(step)

        @pl.when(self.alive(step))
        def _():
            self.hop(shard, head).wait_recv()

            @pl.when(self.passes_on)
            def _():
                self.hop(shard, head).start()

            self.update(shard, head, self.kvbuf.at[shard, head], False)

    def change(self, head):
        return self.a_buf[head, 0] / self.l_buf[head, 0] - self.a_buf[head, 1] / self.l_buf[head, 1]

    def drain(self):
        def body(step, carry):
            @pl.when(self.alive(step) & self.passes_on)
            def _():
                for head in range(self.heads):
                    self.hop(self.shard_at(step), head).wait_send()

            return carry

        lax.fori_loop(0, self.size, body, 0)


def plus_kernel(
    n_head,
    slots,
    hidden,
    wq,
    wk,
    wv,
    out_w,
    sites,
    shift,
    bases,
    embed,
    freq,
    q_out,
    kv_out,
    w_out,
    *rest,
):
    work, sems, (x_send, x_recv, x_own) = rest[:4], rest[4:8], rest[8:]
    z = lax.axis_index("head")
    plane = lax.axis_index("groups") * lax.axis_size("ctx") + lax.axis_index("ctx")
    part, feats = w_out.shape[1], w_out.shape[2]
    part_rows = pl.ds(pl.multiple_of(plane * part, part), part)
    greet_all("head", n_head)
    layer = Layer(
        n_head, slots, 0, hidden, (wq, wk, wv), (sites, shift, bases, embed, freq), work, sems
    )
    layer.open()

    def trade(shift):
        owner = (z + shift) % n_head
        cols = pl.ds(pl.multiple_of(owner * feats, feats), feats)
        return pltpu.make_async_remote_copy(
            src_ref=out_w.at[part_rows, cols],
            dst_ref=w_out.at[z],
            send_sem=x_send.at[owner],
            recv_sem=x_recv.at[z],
            device_id={"head": owner},
            device_id_type=MESH,
        )

    def traded(shift):
        source = (z + shift) % n_head
        cols = pl.ds(pl.multiple_of(z * feats, feats), feats)
        return pltpu.make_async_remote_copy(
            src_ref=out_w.at[part_rows, cols],
            dst_ref=w_out.at[source],
            send_sem=x_send.at[source],
            recv_sem=x_recv.at[source],
            device_id={"head": source},
            device_id_type=MESH,
        )

    for step in range(1, n_head):
        trade(step).start()
    keep = pltpu.make_async_copy(
        out_w.at[part_rows, pl.ds(pl.multiple_of(z * feats, feats), feats)], w_out.at[z], x_own
    )
    loads = layer.load() + [keep]
    keep.start()
    layer.tables()
    for copy in loads:
        copy.wait()
    layer.run()
    layer.finish(q_out, kv_out)
    for step in range(1, n_head):
        traded(step).wait_recv()
        trade(step).wait_send()
    layer.drain()


def minus_kernel(
    n_head,
    n_ctx,
    slots,
    hidden,
    wq,
    wk,
    wv,
    sites,
    shift,
    bases,
    embed,
    freq,
    q_plus,
    kv_plus,
    q_out,
    kv_out,
    change,
    *rest,
):
    work, sems, seen = rest[:4], rest[4:8], rest[8:]
    greet(("head", n_head), ("ctx", n_ctx))
    layer = Layer(
        n_head, slots, 1, hidden, (wq, wk, wv), (sites, shift, bases, embed, freq), work, sems
    )
    attention = Attention(n_ctx, slots, 0, q_plus, kv_plus, sites, seen)
    layer.open()
    for head in range(attention.heads):
        attention.open(head)
    loads = layer.load()
    layer.tables()
    attention.times()

    def own_head(head, carry):
        attention.own_block(head)
        return carry

    lax.fori_loop(0, attention.heads, own_head, 0)
    for copy in loads:
        copy.wait()

    def between(step):
        span = max(n_head - 2, 1)
        low = 1 + jnp.maximum(step - 1, 0) * (n_ctx - 1) // span
        high = 1 + step * (n_ctx - 1) // span
        high = jnp.minimum(high, n_ctx)

        def body(at, carry):
            def each(head, inner):
                attention.arrive(at, head)
                return inner

            return lax.fori_loop(0, attention.heads, each, carry)

        lax.fori_loop(low, high, body, 0)

    layer.run(between)
    layer.finish(q_out, kv_out)
    for head in range(attention.heads):
        change[head] = attention.change(head)
    attention.drain()
    layer.drain()


def last_kernel(
    n_head,
    n_ctx,
    slots,
    q_in,
    kv_in,
    sites,
    change,
    w_in,
    out,
    w_buf,
    gbuf,
    mine,
    total_out,
    w_sem,
    gs_sem,
    gr_sem,
    *seen,
):
    z = lax.axis_index("head")
    greet(("ctx", n_ctx), all_of=("head", n_head))
    attention = Attention(n_ctx, slots, 1, q_in, kv_in, sites, seen)
    heads = attention.heads
    attention.open(0)
    w_load = pltpu.make_async_copy(w_in, w_buf, w_sem)
    w_load.start()
    attention.times()

    def deliver(head, peer, source):
        return pltpu.make_async_remote_copy(
            src_ref=mine.at[head],
            dst_ref=gbuf.at[source, head],
            send_sem=gs_sem.at[peer, head],
            recv_sem=gr_sem.at[source, head],
            device_id={"head": peer},
            device_id_type=MESH,
        )

    def one_head(head, carry):
        attention.open(head + 1)
        attention.own_block(head)

        def body(at, inner):
            attention.arrive(at, head)
            return inner

        lax.fori_loop(1, n_ctx, body, 0)
        mine[head] = (0.5 * (change[head] + attention.change(head))).astype(jnp.bfloat16)
        for step in range(1, n_head):
            deliver(head, (z + step) % n_head, z).start()
        return carry

    lax.fori_loop(0, heads, one_head, 0)
    w_load.wait()

    def joined(source):
        return jnp.concatenate([source[head] for head in range(heads)], axis=1)

    total_out[...] = jnp.dot(joined(mine), w_buf[z], preferred_element_type=jnp.float32)
    shard_of = near_first(z, n_head)

    def gather_step(step, carry):
        shard = shard_of(step)
        for head in range(heads):
            deliver(head, shard, shard).wait_recv()
        total_out[...] += jnp.dot(
            joined(gbuf.at[shard]), w_buf[shard], preferred_element_type=jnp.float32
        )
        return carry

    lax.fori_loop(1, n_head, gather_step, 0)
    out[...] = total_out[...].astype(jnp.bfloat16)

    def drain_gather(step, carry):
        for head in range(heads):
            deliver(head, (z + step) % n_head, z).wait_send()
        return carry

    lax.fori_loop(1, n_head, drain_gather, 0)
    attention.drain()


def vmem():
    return pl.BlockSpec(memory_space=pltpu.VMEM)


def anywhere():
    return pl.BlockSpec(memory_space=pl.ANY)


def shards(
    hidden,
    strand_bases,
    variant_sites,
    base_shift,
    base_embed,
    query_weight,
    key_weight,
    value_weight,
    out_weight,
):
    rows, feats = hidden.shape[1], hidden.shape[2]
    n_head = lax.axis_size("head")
    n_ctx = lax.axis_size("ctx")
    slots = 2 * VAR_DEV
    wide = rows + slots
    width, hw = query_weight.shape
    heads = hw // HEAD_DIM
    part = hw // (lax.axis_size("groups") * n_ctx)

    half = HEAD_DIM // 2
    freq = jnp.power(ROPE_BASE, -jnp.arange(half, dtype=jnp.float32) * 2.0 / HEAD_DIM)
    small = (
        variant_sites[None, :],
        base_shift[None, :],
        strand_bases[None, :],
        base_embed,
        jnp.concatenate([freq, freq])[None, :],
    )
    weights = (query_weight, key_weight, value_weight)
    layer_work = [
        pltpu.VMEM((n_head, rows, feats), jnp.bfloat16),
        pltpu.VMEM((3, width, hw), jnp.bfloat16),
        pltpu.VMEM((wide, feats), jnp.bfloat16),
        pltpu.VMEM((wide, 3 * hw), jnp.float32),
        pltpu.SemaphoreType.DMA(()),
        pltpu.SemaphoreType.DMA((3,)),
        pltpu.SemaphoreType.DMA((2, n_head, PIECES)),
        pltpu.SemaphoreType.DMA((n_head, PIECES)),
    ]
    attend_work = [
        pltpu.VMEM((n_ctx, heads, wide, 2 * HEAD_DIM), jnp.bfloat16),
        pltpu.VMEM((n_ctx, 1, wide), jnp.float32),
        pltpu.VMEM((heads, 2, rows, 1), jnp.float32),
        pltpu.VMEM((heads, 2, rows, 1), jnp.float32),
        pltpu.VMEM((heads, 2, rows, HEAD_DIM), jnp.float32),
        pltpu.SemaphoreType.DMA((n_ctx, heads)),
        pltpu.SemaphoreType.DMA((n_ctx, heads)),
    ]
    q_shape = jax.ShapeDtypeStruct((2, rows, hw), jnp.bfloat16)
    kv_shape = jax.ShapeDtypeStruct((heads, wide, 2 * HEAD_DIM), jnp.bfloat16)

    def call(kernel, number, out_shape, in_specs, scratch, name):
        return pl.pallas_call(
            kernel,
            out_shape=out_shape,
            in_specs=in_specs,
            out_specs=jax.tree.map(lambda _: vmem(), out_shape),
            scratch_shapes=scratch,
            compiler_params=pltpu.CompilerParams(
                collective_id=number, has_side_effects=True, vmem_limit_bytes=VMEM_LIMIT
            ),
            name=name,
        )

    q_plus, kv_plus, w_mine = call(
        functools.partial(plus_kernel, n_head, slots),
        0,
        (q_shape, kv_shape, jax.ShapeDtypeStruct((n_head, part, feats), jnp.bfloat16)),
        [anywhere()] * 5 + [vmem()] * 5,
        layer_work
        + [
            pltpu.SemaphoreType.DMA((n_head,)),
            pltpu.SemaphoreType.DMA((n_head,)),
            pltpu.SemaphoreType.DMA(()),
        ],
        "project_plus",
    )(hidden, *weights, out_weight, *small)
    w_all = lax.all_gather(w_mine, ("groups", "ctx"), axis=1, tiled=True)
    q_minus, kv_minus, change = call(
        functools.partial(minus_kernel, n_head, n_ctx, slots),
        1,
        (q_shape, kv_shape, jax.ShapeDtypeStruct((heads, rows, HEAD_DIM), jnp.float32)),
        [anywhere()] * 4 + [vmem()] * 7,
        layer_work + attend_work,
        "attend_plus",
    )(hidden, *weights, *small, q_plus, kv_plus)
    return call(
        functools.partial(last_kernel, n_head, n_ctx, slots),
        2,
        jax.ShapeDtypeStruct((rows, feats), jnp.bfloat16),
        [vmem()] * 4 + [anywhere()],
        [
            pltpu.VMEM((n_head, hw, feats), jnp.bfloat16),
            pltpu.VMEM((n_head, heads, rows, HEAD_DIM), jnp.bfloat16),
            pltpu.VMEM((heads, rows, HEAD_DIM), jnp.bfloat16),
            pltpu.VMEM((rows, feats), jnp.float32),
            pltpu.SemaphoreType.DMA(()),
            pltpu.SemaphoreType.DMA((n_head, heads)),
            pltpu.SemaphoreType.DMA((n_head, heads)),
        ]
        + attend_work,
        "attend_minus",
    )(q_minus, kv_minus, small[0], change, w_all)


def solution(mesh):
    return jax.shard_map(
        shards,
        mesh=mesh,
        in_specs=(
            P(None, ("groups", "ctx"), "head"),
            P(("groups", "ctx")),
            P("groups"),
            P("groups"),
            P(),
            P(None, "head"),
            P(None, "head"),
            P(None, "head"),
            P("head", None),
        ),
        out_specs=P(("groups", "ctx"), "head"),
        check_vma=False,
    )
```

```python
import functools
import math

import jax
import jax.numpy as jnp
from jax import lax
from jax.experimental import pallas as pl
from jax.experimental.pallas import tpu as pltpu
from jax.sharding import PartitionSpec as P

HEAD_DIM = 128
VAR_DEV = 32
ROPE_BASE = 10000.0
NEG_FILL = -1e30
FAR = float(1 << 29)
PIECES = 2
MESH = pl.DeviceIdType.MESH
VMEM_LIMIT = 60 * 1024 * 1024


def greet(*axes, all_of=None):
    barrier = pltpu.get_barrier_semaphore()
    peers = 0
    for axis, size in axes:
        me = lax.axis_index(axis)

        @pl.when(me > 0)
        def _():
            pl.semaphore_signal(barrier, inc=1, device_id={axis: me - 1}, device_id_type=MESH)

        @pl.when(me < size - 1)
        def _():
            pl.semaphore_signal(barrier, inc=1, device_id={axis: me + 1}, device_id_type=MESH)

        peers = peers + jnp.minimum(me, 1) + jnp.minimum(size - 1 - me, 1)
    if all_of is not None:
        axis, size = all_of
        me = lax.axis_index(axis)
        for shift in range(1, size):
            pl.semaphore_signal(
                barrier, inc=1, device_id={axis: (me + shift) % size}, device_id_type=MESH
            )
        peers = peers + size - 1
    pl.semaphore_wait(barrier, peers)


def greet_all(axis, size):
    me = lax.axis_index(axis)
    barrier = pltpu.get_barrier_semaphore()
    for shift in range(1, size):
        pl.semaphore_signal(
            barrier, inc=1, device_id={axis: (me + shift) % size}, device_id_type=MESH
        )
    pl.semaphore_wait(barrier, size - 1)


def iota(shape, axis):
    return lax.broadcasted_iota(jnp.int32, shape, axis).astype(jnp.float32)


def to_column(row):
    size = row.shape[1]
    eye = iota((size, 1), 0) == iota((1, size), 1)
    return jnp.sum(jnp.where(eye, row, 0.0), axis=1, keepdims=True)


def slot_of(sites_row, sites_col, begin, rows):
    count = sites_row.shape[1]

    def inside(sites):
        return jnp.where((sites >= begin) & (sites < begin + rows), 1.0, 0.0)

    in_row, in_col = inside(sites_row), inside(sites_col)
    at_row, at_col = iota((1, count), 1), iota((count, 1), 0)
    rank_col = jnp.sum(jnp.where(at_row < at_col, in_row, 0.0), axis=1, keepdims=True)
    rank_row = jnp.sum(jnp.where(at_col < at_row, in_col, 0.0), axis=0, keepdims=True)
    return (
        jnp.where(in_row > 0.5, rank_row, -1.0),
        jnp.where(in_col > 0.5, rank_col, -1.0),
    )


def slot_row(slot_col, sites_col, slots):
    match = slot_col == iota((1, slots), 1)
    place = jnp.sum(jnp.where(match, sites_col, 0.0), axis=0, keepdims=True)
    live = jnp.sum(jnp.where(match, 1.0, 0.0), axis=0, keepdims=True)
    return place, live


def near_first(z, size):
    shorter = jnp.minimum(z, size - 1 - z)
    long_side = jnp.where(z < size - 1 - z, 1, -1)

    def shard_of(step):
        paired = jnp.where(step % 2 == 1, (step + 1) // 2, -((step + 1) // 2))
        return z + jnp.where(step <= 2 * shorter, paired, long_side * (step - shorter))

    return shard_of


class Layer:
    def __init__(self, size, slots, strand, hidden, weights, small, work, sems):
        self.size, self.slots, self.strand = size, slots, strand
        self.hidden, self.weights = hidden, weights
        self.sites, self.shift, self.bases, self.embed, self.freq = small
        self.xbuf, self.wbuf, self.stk, self.acc = work
        self.own_sem, self.w_sem, self.s_sem, self.r_sem = sems
        self.z = lax.axis_index("head")
        self.rows, self.feats = hidden.shape[1], hidden.shape[2]
        self.hw = weights[0].shape[1]
        self.piece = self.rows // PIECES
        self.shard_of = near_first(self.z, size)

    def hop(self, side, shard, part, own=False):
        span = pl.ds(part * self.piece, self.piece)
        return pltpu.make_async_remote_copy(
            src_ref=self.hidden.at[self.strand, span] if own else self.xbuf.at[shard, span],
            dst_ref=self.xbuf.at[shard, span],
            send_sem=self.s_sem.at[side, shard, part],
            recv_sem=self.r_sem.at[shard, part],
            device_id={"head": self.z - 1 if side == 0 else self.z + 1},
            device_id_type=MESH,
        )

    def open(self):
        z = self.z
        for part in range(PIECES):

            @pl.when(z > 0)
            def _():
                self.hop(0, z, part, True).start()

            @pl.when(z < self.size - 1)
            def _():
                self.hop(1, z, part, True).start()

    def load(self):
        copies = [
            pltpu.make_async_copy(
                self.hidden.at[self.strand], self.xbuf.at[self.z], self.own_sem
            )
        ] + [
            pltpu.make_async_copy(weight, self.wbuf.at[index], self.w_sem.at[index])
            for index, weight in enumerate(self.weights)
        ]
        for copy in copies:
            copy.start()
        return copies

    def tables(self):
        rows, slots = self.rows, self.slots
        me = lax.axis_index("ctx")
        begin = (me * rows).astype(jnp.float32)
        window = rows * lax.axis_size("ctx")
        sites_row = self.sites[...].astype(jnp.float32)
        sites_col = to_column(sites_row)
        slot_r, slot_c = slot_of(sites_row, sites_col, begin, rows)
        place_r, live_r = slot_row(slot_c, sites_col, slots)
        match_t = iota((slots, 1), 0) == slot_r
        place_c = jnp.sum(jnp.where(match_t, sites_row, 0.0), axis=1, keepdims=True)
        self.live = jnp.sum(jnp.where(match_t, 1.0, 0.0), axis=1, keepdims=True)
        shift = jnp.sum(
            jnp.where(match_t, self.shift[...].astype(jnp.float32), 0.0), axis=1, keepdims=True
        )
        local_c = jnp.where(self.live > 0.5, place_c - begin, -1.0)
        local_r = jnp.where(live_r > 0.5, place_r - begin, -1.0)
        hit = local_c == iota((1, rows), 1)
        hit_t = iota((rows, 1), 0) == local_r
        self.sel = jnp.where(hit, 1.0, 0.0).astype(jnp.bfloat16)
        spread = jnp.where(hit_t, 1.0, 0.0)
        self.sel_t = spread.astype(jnp.bfloat16)
        self.has_row = jnp.sum(spread, axis=1, keepdims=True)
        old = jnp.sum(
            jnp.where(hit, self.bases[...].astype(jnp.float32), 0.0), axis=1, keepdims=True
        )
        new = old + shift
        new = jnp.where(new >= 4.0, new - 4.0, new)
        if self.strand == 1:
            old, new = 3.0 - old, 3.0 - new
        self.coefs = [
            jnp.where(
                self.live > 0.5,
                jnp.where(new == code, 1.0, 0.0) - jnp.where(old == code, 1.0, 0.0),
                0.0,
            )
            for code in range(4)
        ]
        place = jnp.concatenate([begin + iota((rows, 1), 0), place_c], axis=0)
        if self.strand == 1:
            place = window - 1 - place
        angle = place * self.freq[...]
        self.cos = jnp.cos(angle)
        side = jnp.where(iota((1, HEAD_DIM), 1) < HEAD_DIM // 2, -1.0, 1.0)
        self.sin = jnp.sin(angle) * side

    def run(self, between=None):
        z, size, rows, feats, hw = self.z, self.size, self.rows, self.feats, self.hw
        self.acc[...] = jnp.zeros_like(self.acc)

        def step_body(step, carry):
            shard = self.shard_of(step)
            for part in range(PIECES):

                @pl.when(shard > z)
                def _():
                    self.hop(0, shard, part).wait_recv()

                    @pl.when(z > 0)
                    def _():
                        self.hop(0, shard, part).start()

                @pl.when(shard < z)
                def _():
                    self.hop(1, shard, part).wait_recv()

                    @pl.when(z < size - 1)
                    def _():
                        self.hop(1, shard, part).start()

            block = self.xbuf[shard]
            self.stk[pl.ds(0, rows), :] = block
            first = pl.multiple_of(shard * feats, feats)
            letters = self.embed[:, pl.ds(first, feats)].astype(jnp.float32)
            diff = sum(self.coefs[code] * letters[code : code + 1] for code in range(4))
            picked = jnp.dot(self.sel, block, preferred_element_type=jnp.float32)
            self.stk[pl.ds(rows, self.slots), :] = (picked + diff).astype(jnp.bfloat16)
            for index in range(3):
                self.acc[:, pl.ds(index * hw, hw)] += jnp.dot(
                    self.stk[...],
                    self.wbuf[index, pl.ds(first, feats), :],
                    preferred_element_type=jnp.float32,
                )
            if between is not None:
                between(step)
            return carry

        lax.fori_loop(0, size, step_body, 0)

    def finish(self, q_out, kv_out):
        rows, hw = self.rows, self.hw
        for head in range(hw // HEAD_DIM):
            cols = pl.ds(head * HEAD_DIM, HEAD_DIM)
            for index in range(2):
                raw = self.acc[:, pl.ds(index * hw + head * HEAD_DIM, HEAD_DIM)]
                turned = raw * self.cos + pltpu.roll(raw, HEAD_DIM // 2, 1) * self.sin
                turned = turned.astype(jnp.bfloat16)
                if index == 0:
                    base = turned[:rows]
                    placed = jnp.dot(
                        self.sel_t, turned[rows:], preferred_element_type=jnp.float32
                    )
                    q_out[0, :, cols] = base
                    q_out[1, :, cols] = jnp.where(
                        self.has_row > 0.5, placed, base.astype(jnp.float32)
                    ).astype(jnp.bfloat16)
                else:
                    kv_out[head, :, pl.ds(0, HEAD_DIM)] = turned
            kv_out[head, :, pl.ds(HEAD_DIM, HEAD_DIM)] = self.acc[
                :, pl.ds(2 * hw + head * HEAD_DIM, HEAD_DIM)
            ].astype(jnp.bfloat16)

    def drain(self):
        z = self.z

        def body(step, carry):
            shard = self.shard_of(step)
            for part in range(PIECES):

                @pl.when((shard >= z) & (z > 0))
                def _():
                    self.hop(0, shard, part).wait_send()

                @pl.when((shard <= z) & (z < self.size - 1))
                def _():
                    self.hop(1, shard, part).wait_send()

            return carry

        lax.fori_loop(0, self.size, body, 0)


class Attention:
    def __init__(self, size, slots, strand, q_in, kv_in, sites, work):
        self.size, self.slots, self.strand = size, slots, strand
        self.q_in, self.kv_in = q_in, kv_in
        self.kvbuf, self.kt_buf, self.m_buf, self.l_buf, self.a_buf = work[:5]
        self.s_sem, self.r_sem = work[5:]
        self.me = lax.axis_index("ctx")
        self.rows, self.hw = q_in.shape[1], q_in.shape[2]
        self.heads = self.hw // HEAD_DIM
        self.window = self.rows * size
        self.passes_on = self.me < size - 1 if strand == 0 else self.me > 0
        self.sites_row = sites[...].astype(jnp.float32)
        self.sites_col = to_column(self.sites_row)

    def hop(self, shard, head, own=False):
        return pltpu.make_async_remote_copy(
            src_ref=self.kv_in.at[head] if own else self.kvbuf.at[shard, head],
            dst_ref=self.kvbuf.at[shard, head],
            send_sem=self.s_sem.at[shard, head],
            recv_sem=self.r_sem.at[shard, head],
            device_id={"ctx": self.me + 1 if self.strand == 0 else self.me - 1},
            device_id_type=MESH,
        )

    def open(self, head):
        @pl.when(self.passes_on & (head < self.heads))
        def _():
            self.hop(self.me, head, True).start()

    def clock(self, place):
        return place if self.strand == 0 else self.window - 1 - place

    def times(self):
        rows, slots = self.rows, self.slots

        def body(shard, carry):
            begin = (shard * rows).astype(jnp.float32)
            place = begin + iota((1, rows), 1)
            _, slot_c = slot_of(self.sites_row, self.sites_col, begin, rows)
            slot_place, live = slot_row(slot_c, self.sites_col, slots)
            taken = jnp.sum(
                jnp.where(self.sites_col == place, 1.0, 0.0), axis=0, keepdims=True
            )
            self.kt_buf[shard] = jnp.concatenate(
                [
                    jnp.where(taken > 0.5, FAR, self.clock(place)),
                    jnp.where(live > 0.5, self.clock(slot_place), FAR),
                ],
                axis=1,
            )
            return carry

        lax.fori_loop(0, self.size, body, 0)

    def update(self, shard, head, block, first):
        rows, slots = self.rows, self.slots
        q_time = self.clock((self.me * rows).astype(jnp.float32) + iota((rows, 1), 0))
        ref_time = self.clock((shard * rows).astype(jnp.float32) + iota((1, rows), 1))
        k_times = (ref_time, self.kt_buf[shard])
        spans = (rows, rows + slots)
        log_scale = math.log2(math.e) / math.sqrt(HEAD_DIM)
        cols = pl.ds(pl.multiple_of(head * HEAD_DIM, HEAD_DIM), HEAD_DIM)
        for kind in range(2):
            span = pl.ds(0, spans[kind])
            raw = lax.dot_general(
                self.q_in[kind, :, cols],
                block[span, pl.ds(0, HEAD_DIM)],
                (((1,), (1,)), ((), ())),
                preferred_element_type=jnp.float32,
            )
            if first:
                raw = jnp.where(k_times[kind] <= q_time, raw, NEG_FILL)
            elif kind == 1:
                raw = raw + jnp.where(k_times[1] >= FAR, NEG_FILL, 0.0)
            top = jnp.max(raw, axis=1, keepdims=True)
            if not first:
                old = self.m_buf[head, kind]
                top = jnp.maximum(old, top)
                fade = jnp.exp2((old - top) * log_scale)
            weights = jnp.exp2((raw - top) * log_scale)
            values = block[span, pl.ds(HEAD_DIM, HEAD_DIM)]
            both = jnp.dot(
                weights.astype(jnp.bfloat16),
                jnp.concatenate([values, jnp.ones_like(values)], axis=1),
                preferred_element_type=jnp.float32,
            )
            vec, total = both[:, :HEAD_DIM], both[:, HEAD_DIM:]
            if not first:
                total = total + fade * self.l_buf[head, kind]
                vec = vec + fade * self.a_buf[head, kind]
            self.m_buf[head, kind] = top
            self.l_buf[head, kind] = total
            self.a_buf[head, kind] = vec

    def own_block(self, head):
        self.update(self.me, head, self.kv_in.at[head], True)

    def shard_at(self, step):
        return self.me - step if self.strand == 0 else self.me + step

    def alive(self, step):
        shard = self.shard_at(step)
        return shard >= 0 if self.strand == 0 else shard < self.size

    def arrive(self, step, head):
        shard = self.shard_at(step)

        @pl.when(self.alive(step))
        def _():
            self.hop(shard, head).wait_recv()

            @pl.when(self.passes_on)
            def _():
                self.hop(shard, head).start()

            self.update(shard, head, self.kvbuf.at[shard, head], False)

    def change(self, head):
        return self.a_buf[head, 0] / self.l_buf[head, 0] - self.a_buf[head, 1] / self.l_buf[head, 1]

    def drain(self):
        def body(step, carry):
            @pl.when(self.alive(step) & self.passes_on)
            def _():
                for head in range(self.heads):
                    self.hop(self.shard_at(step), head).wait_send()

            return carry

        lax.fori_loop(0, self.size, body, 0)


def plus_kernel(
    n_head,
    slots,
    hidden,
    wq,
    wk,
    wv,
    out_w,
    sites,
    shift,
    bases,
    embed,
    freq,
    q_out,
    kv_out,
    w_out,
    *rest,
):
    work, sems, (x_send, x_recv, x_own) = rest[:4], rest[4:8], rest[8:]
    z = lax.axis_index("head")
    plane = lax.axis_index("groups") * lax.axis_size("ctx") + lax.axis_index("ctx")
    part, feats = w_out.shape[1], w_out.shape[2]
    part_rows = pl.ds(pl.multiple_of(plane * part, part), part)
    greet_all("head", n_head)
    layer = Layer(
        n_head, slots, 0, hidden, (wq, wk, wv), (sites, shift, bases, embed, freq), work, sems
    )
    layer.open()

    def trade(shift):
        owner = (z + shift) % n_head
        cols = pl.ds(pl.multiple_of(owner * feats, feats), feats)
        return pltpu.make_async_remote_copy(
            src_ref=out_w.at[part_rows, cols],
            dst_ref=w_out.at[z],
            send_sem=x_send.at[owner],
            recv_sem=x_recv.at[z],
            device_id={"head": owner},
            device_id_type=MESH,
        )

    def traded(shift):
        source = (z + shift) % n_head
        cols = pl.ds(pl.multiple_of(z * feats, feats), feats)
        return pltpu.make_async_remote_copy(
            src_ref=out_w.at[part_rows, cols],
            dst_ref=w_out.at[source],
            send_sem=x_send.at[source],
            recv_sem=x_recv.at[source],
            device_id={"head": source},
            device_id_type=MESH,
        )

    for step in range(1, n_head):
        trade(step).start()
    keep = pltpu.make_async_copy(
        out_w.at[part_rows, pl.ds(pl.multiple_of(z * feats, feats), feats)], w_out.at[z], x_own
    )
    loads = layer.load() + [keep]
    keep.start()
    layer.tables()
    for copy in loads:
        copy.wait()
    layer.run()
    layer.finish(q_out, kv_out)
    for step in range(1, n_head):
        traded(step).wait_recv()
        trade(step).wait_send()
    layer.drain()


def minus_kernel(
    n_head,
    n_ctx,
    slots,
    hidden,
    wq,
    wk,
    wv,
    sites,
    shift,
    bases,
    embed,
    freq,
    q_plus,
    kv_plus,
    q_out,
    kv_out,
    change,
    *rest,
):
    work, sems, seen = rest[:4], rest[4:8], rest[8:]
    greet(("head", n_head), ("ctx", n_ctx))
    layer = Layer(
        n_head, slots, 1, hidden, (wq, wk, wv), (sites, shift, bases, embed, freq), work, sems
    )
    attention = Attention(n_ctx, slots, 0, q_plus, kv_plus, sites, seen)
    layer.open()
    for head in range(attention.heads):
        attention.open(head)
    loads = layer.load()
    layer.tables()
    attention.times()

    def own_head(head, carry):
        attention.own_block(head)
        return carry

    lax.fori_loop(0, attention.heads, own_head, 0)
    for copy in loads:
        copy.wait()

    def between(step):
        span = max(n_head - 2, 1)
        low = 1 + jnp.maximum(step - 1, 0) * (n_ctx - 1) // span
        high = 1 + step * (n_ctx - 1) // span
        high = jnp.minimum(high, n_ctx)

        def body(at, carry):
            def each(head, inner):
                attention.arrive(at, head)
                return inner

            return lax.fori_loop(0, attention.heads, each, carry)

        lax.fori_loop(low, high, body, 0)

    layer.run(between)
    layer.finish(q_out, kv_out)
    for head in range(attention.heads):
        change[head] = attention.change(head)
    attention.drain()
    layer.drain()


def last_kernel(
    n_head,
    n_ctx,
    slots,
    q_in,
    kv_in,
    sites,
    change,
    w_in,
    out,
    w_buf,
    gbuf,
    mine,
    total_out,
    w_sem,
    gs_sem,
    gr_sem,
    *seen,
):
    z = lax.axis_index("head")
    greet(("ctx", n_ctx), all_of=("head", n_head))
    attention = Attention(n_ctx, slots, 1, q_in, kv_in, sites, seen)
    heads = attention.heads
    attention.open(0)
    w_load = pltpu.make_async_copy(w_in, w_buf, w_sem)
    w_load.start()
    attention.times()

    def deliver(head, peer, source):
        return pltpu.make_async_remote_copy(
            src_ref=mine.at[head],
            dst_ref=gbuf.at[source, head],
            send_sem=gs_sem.at[peer, head],
            recv_sem=gr_sem.at[source, head],
            device_id={"head": peer},
            device_id_type=MESH,
        )

    def one_head(head, carry):
        attention.open(head + 1)
        attention.own_block(head)

        def body(at, inner):
            attention.arrive(at, head)
            return inner

        lax.fori_loop(1, n_ctx, body, 0)
        mine[head] = (0.5 * (change[head] + attention.change(head))).astype(jnp.bfloat16)
        for step in range(1, n_head):
            deliver(head, (z + step) % n_head, z).start()
        return carry

    lax.fori_loop(0, heads, one_head, 0)
    w_load.wait()

    def joined(source):
        return jnp.concatenate([source[head] for head in range(heads)], axis=1)

    total_out[...] = jnp.dot(joined(mine), w_buf[z], preferred_element_type=jnp.float32)
    shard_of = near_first(z, n_head)

    def gather_step(step, carry):
        shard = shard_of(step)
        for head in range(heads):
            deliver(head, shard, shard).wait_recv()
        total_out[...] += jnp.dot(
            joined(gbuf.at[shard]), w_buf[shard], preferred_element_type=jnp.float32
        )
        return carry

    lax.fori_loop(1, n_head, gather_step, 0)
    out[...] = total_out[...].astype(jnp.bfloat16)

    def drain_gather(step, carry):
        for head in range(heads):
            deliver(head, (z + step) % n_head, z).wait_send()
        return carry

    lax.fori_loop(1, n_head, drain_gather, 0)
    attention.drain()


def vmem():
    return pl.BlockSpec(memory_space=pltpu.VMEM)


def anywhere():
    return pl.BlockSpec(memory_space=pl.ANY)


def shards(
    hidden,
    strand_bases,
    variant_sites,
    base_shift,
    base_embed,
    query_weight,
    key_weight,
    value_weight,
    out_weight,
):
    rows, feats = hidden.shape[1], hidden.shape[2]
    n_head = lax.axis_size("head")
    n_ctx = lax.axis_size("ctx")
    slots = 2 * VAR_DEV
    wide = rows + slots
    width, hw = query_weight.shape
    heads = hw // HEAD_DIM
    part = hw // (lax.axis_size("groups") * n_ctx)

    half = HEAD_DIM // 2
    freq = jnp.power(ROPE_BASE, -jnp.arange(half, dtype=jnp.float32) * 2.0 / HEAD_DIM)
    small = (
        variant_sites[None, :],
        base_shift[None, :],
        strand_bases[None, :],
        base_embed,
        jnp.concatenate([freq, freq])[None, :],
    )
    weights = (query_weight, key_weight, value_weight)
    layer_work = [
        pltpu.VMEM((n_head, rows, feats), jnp.bfloat16),
        pltpu.VMEM((3, width, hw), jnp.bfloat16),
        pltpu.VMEM((wide, feats), jnp.bfloat16),
        pltpu.VMEM((wide, 3 * hw), jnp.float32),
        pltpu.SemaphoreType.DMA(()),
        pltpu.SemaphoreType.DMA((3,)),
        pltpu.SemaphoreType.DMA((2, n_head, PIECES)),
        pltpu.SemaphoreType.DMA((n_head, PIECES)),
    ]
    attend_work = [
        pltpu.VMEM((n_ctx, heads, wide, 2 * HEAD_DIM), jnp.bfloat16),
        pltpu.VMEM((n_ctx, 1, wide), jnp.float32),
        pltpu.VMEM((heads, 2, rows, 1), jnp.float32),
        pltpu.VMEM((heads, 2, rows, HEAD_DIM), jnp.float32),
        pltpu.VMEM((heads, 2, rows, HEAD_DIM), jnp.float32),
        pltpu.SemaphoreType.DMA((n_ctx, heads)),
        pltpu.SemaphoreType.DMA((n_ctx, heads)),
    ]
    q_shape = jax.ShapeDtypeStruct((2, rows, hw), jnp.bfloat16)
    kv_shape = jax.ShapeDtypeStruct((heads, wide, 2 * HEAD_DIM), jnp.bfloat16)

    def call(kernel, number, out_shape, in_specs, scratch, name):
        return pl.pallas_call(
            kernel,
            out_shape=out_shape,
            in_specs=in_specs,
            out_specs=jax.tree.map(lambda _: vmem(), out_shape),
            scratch_shapes=scratch,
            compiler_params=pltpu.CompilerParams(
                collective_id=number, has_side_effects=True, vmem_limit_bytes=VMEM_LIMIT
            ),
            name=name,
        )

    q_plus, kv_plus, w_mine = call(
        functools.partial(plus_kernel, n_head, slots),
        0,
        (q_shape, kv_shape, jax.ShapeDtypeStruct((n_head, part, feats), jnp.bfloat16)),
        [anywhere()] * 5 + [vmem()] * 5,
        layer_work
        + [
            pltpu.SemaphoreType.DMA((n_head,)),
            pltpu.SemaphoreType.DMA((n_head,)),
            pltpu.SemaphoreType.DMA(()),
        ],
        "project_plus",
    )(hidden, *weights, out_weight, *small)
    w_all = lax.all_gather(w_mine, ("groups", "ctx"), axis=1, tiled=True)
    q_minus, kv_minus, change = call(
        functools.partial(minus_kernel, n_head, n_ctx, slots),
        1,
        (q_shape, kv_shape, jax.ShapeDtypeStruct((heads, rows, HEAD_DIM), jnp.float32)),
        [anywhere()] * 4 + [vmem()] * 7,
        layer_work + attend_work,
        "attend_plus",
    )(hidden, *weights, *small, q_plus, kv_plus)
    return call(
        functools.partial(last_kernel, n_head, n_ctx, slots),
        2,
        jax.ShapeDtypeStruct((rows, feats), jnp.bfloat16),
        [vmem()] * 4 + [anywhere()],
        [
            pltpu.VMEM((n_head, hw, feats), jnp.bfloat16),
            pltpu.VMEM((n_head, heads, rows, HEAD_DIM), jnp.bfloat16),
            pltpu.VMEM((heads, rows, HEAD_DIM), jnp.bfloat16),
            pltpu.VMEM((rows, feats), jnp.float32),
            pltpu.SemaphoreType.DMA(()),
            pltpu.SemaphoreType.DMA((n_head, heads)),
            pltpu.SemaphoreType.DMA((n_head, heads)),
        ]
        + attend_work,
        "attend_minus",
    )(q_minus, kv_minus, small[0], change, w_all)


def solution(mesh):
    return jax.shard_map(
        shards,
        mesh=mesh,
        in_specs=(
            P(None, ("groups", "ctx"), "head"),
            P(("groups", "ctx")),
            P("groups"),
            P("groups"),
            P(),
            P(None, "head"),
            P(None, "head"),
            P(None, "head"),
            P("head", None),
        ),
        out_specs=P(("groups", "ctx"), "head"),
        check_vma=False,
    )
```
